512 devices in a mesh: ta: 8 (over y), gz: 8 (over x, core), xy: 8 (over z).
Axes of the slice: x: 4, y: 8, z: 8, core: 2. Of those that a mesh axis runs over, the one named last changes fastest.
Arguments:
- right_side: float32 [8, 8, 8, 2, 32, 128], P('ta', 'gz', 'xy'), may hold values from -40 to 40
- stencil: float32 [8, 8, 8, 2, 9, 128, 128], P('ta', 'gz', 'xy'), may hold values from -0.5 to 1.5, as said below
- restrict: float32 [8, 8, 8, 2, 32, 128], P('ta', 'gz', 'xy'), may hold values from -0.5 to 0.5
- aggregate: int32 [8, 8, 8, 2], P('ta', 'gz', 'xy'), may hold values from 0 to 63, as said below
- coarsest_inverse: float32 [2048, 2048], P('xy'), may hold values from -0.125 to 0.125
Outputs:
- solution: float32 [8, 8, 8, 2, 32, 128], P('ta', 'gz', 'xy')
- residual: float32 [8, 8, 8, 2, 32, 128], P('ta', 'gz', 'xy')
The draws below stay inside these ranges and needn't reach their ends.
Inputs may be any that keep to these rules, and one draw needn't show every extreme that they name: `aggregate`: sites are grouped into 2 x 2 x 2 x 2 blocks aligned at even coordinates; each block forms one coarsest site, and the coarsest sites are numbered in an order drawn from the seed. `stencil`: each self block is close to the identity; the other blocks are small and full.
All inputs are finite; a program needn't handle non-finite values.
Results may differ from the reference program's by a relative error of at most 0.0001.
Values sent between devices are 32-bit elements; how exact they have to be, the bound alone decides.
No kernel may reach another device: no remote copies, remote signals or barrier semaphores. Data moves between devices by JAX's collectives and lax.ppermute only.
A program may use at most 64 MiB of HBM per device.

```python
import jax
import jax.numpy as jnp
from jax import lax

C = 128
K3 = 32
NRHS = 32
X_LOC = 2
NT = 8
NZ = 8
NY = 8
NS = 1024
NA = 64
NC3 = 2048


def draw_stencil(key, part):
    noise_key = jax.random.fold_in(key, 11)
    shape = (NT, NZ, NY, X_LOC, 9, C, C)
    noise = jnp.clip(jax.random.normal(noise_key, shape, jnp.float32), -4.0, 4.0)
    noise = noise * (0.3 / C ** 0.5)
    rows = lax.broadcasted_iota(jnp.int32, shape, 5)
    cols = lax.broadcasted_iota(jnp.int32, shape, 6)
    blocks = lax.broadcasted_iota(jnp.int32, shape, 4)
    ident = jnp.where((rows == cols) & (blocks == 0), 1.0, 0.0).astype(jnp.float32)
    return (ident + noise).astype(jnp.float32)


def draw_right_side(key, part):
    base_key = jax.random.fold_in(key, 21)
    scale_key = jax.random.fold_in(key, 22)
    shape = (NT, NZ, NY, X_LOC, NRHS, C)
    values = jnp.clip(jax.random.normal(base_key, shape, jnp.float32), -4.0, 4.0)
    small = (NT, NZ, NY, X_LOC, NRHS, 1)
    tpos = lax.broadcasted_iota(jnp.int32, small, 0)
    zpos = lax.broadcasted_iota(jnp.int32, small, 1)
    ypos = lax.broadcasted_iota(jnp.int32, small, 2)
    xpos = lax.broadcasted_iota(jnp.int32, small, 3)
    flat = ((tpos * NZ + zpos) * NY + ypos) * X_LOC + xpos
    rising = jnp.exp(jnp.log(3.0) * flat.astype(jnp.float32) / (NS - 1))
    spread = jax.random.uniform(scale_key, small, jnp.float32, -0.5, 0.5)
    return (values * rising * jnp.exp(jnp.log(10.0) * spread)).astype(jnp.float32)


def draw_aggregate(key, part):
    perm_key = jax.random.fold_in(key, 31)
    labels = jax.random.permutation(perm_key, NA).astype(jnp.int32)
    shape = (NT, NZ, NY, X_LOC)
    tpos = lax.broadcasted_iota(jnp.int32, shape, 0) // 2
    zpos = lax.broadcasted_iota(jnp.int32, shape, 1) // 2
    ypos = lax.broadcasted_iota(jnp.int32, shape, 2) // 2
    xpos = lax.broadcasted_iota(jnp.int32, shape, 3) // 2
    block = ((tpos * (NZ // 2) + zpos) * (NY // 2) + ypos) * (X_LOC // 2) + xpos
    return labels[block].astype(jnp.int32)


def shard_levels(key, shape, pieces, least, high):
    level, own = 1.0, jax.random.fold_in(key, 6)
    for dim, shards_of in pieces:
        heights = jnp.exp(jax.random.uniform(jax.random.fold_in(own, dim), (shards_of,), jnp.float32, least / len(pieces), high / len(pieces)))
        level = level * jnp.repeat(heights, shape[dim] // shards_of).reshape([-1 if axis == dim else 1 for axis in range(len(shape))])
    return level


def gaussian(key, shape, scale, bound, cuts=(), kind=jnp.bfloat16):
    drawn = scale * jax.random.normal(key, shape, jnp.float32)
    if cuts:
        drawn = drawn * shard_levels(key, shape, cuts, -0.22, 0.18)
    return jnp.clip(drawn, -bound, bound).astype(kind)


def setup_inputs(seed: int = 0) -> dict:
    key_list = jax.random.split(jax.random.key(seed), 6)
    right_side = draw_right_side(jax.random.fold_in(key_list[5], 71), 0)
    stencil = draw_stencil(jax.random.fold_in(key_list[5], 71), 0)
    restrict = gaussian(key_list[2], (NT, NZ, NY, X_LOC, K3, C), C ** -0.5, 0.5, ((0, 8), (1, 8), (2, 8)), jnp.float32)
    aggregate = draw_aggregate(jax.random.fold_in(key_list[5], 71), 0)
    coarsest_inverse = gaussian(key_list[4], (NC3, NC3), NC3 ** -0.5, 0.125, ((0, 8),), jnp.float32)
    return {"right_side": right_side, "stencil": stencil, "restrict": restrict, "aggregate": aggregate, "coarsest_inverse": coarsest_inverse}


def apply_operator(field, stencil):
    shifted = [field,
               jnp.roll(field, -1, 0), jnp.roll(field, 1, 0),
               jnp.roll(field, -1, 1), jnp.roll(field, 1, 1),
               jnp.roll(field, -1, 2), jnp.roll(field, 1, 2),
               jnp.roll(field, -1, 3), jnp.roll(field, 1, 3)]
    result = jnp.zeros(field.shape, jnp.float32)
    for offset in range(9):
        result = result + jnp.einsum("tzyxij,tzyxrj->tzyxri", stencil[:, :, :, :, offset], shifted[offset],
                                     precision=lax.Precision.HIGHEST)
    return result


def inner_sum(one_side, other_side):
    return jnp.sum(one_side * other_side, axis=(0, 1, 2, 3, 5))


def reference(right_side, stencil, restrict, aggregate, coarsest_inverse):
    image_first = apply_operator(right_side, stencil)
    step_first = inner_sum(image_first, right_side) / inner_sum(image_first, image_first)
    resid_mid = right_side - step_first[:, None] * image_first
    image_raw = apply_operator(resid_mid, stencil)
    beta = inner_sum(image_first, image_raw) / inner_sum(image_first, image_first)
    image_second = image_raw - beta[:, None] * image_first
    direction = resid_mid - beta[:, None] * right_side
    step_second = inner_sum(image_second, resid_mid) / inner_sum(image_second, image_second)
    solution_gcr = step_first[:, None] * right_side + step_second[:, None] * direction
    residual = resid_mid - step_second[:, None] * image_second
    restricted = jnp.einsum("tzyxkc,tzyxrc->tzyxrk", restrict, residual, precision=lax.Precision.HIGHEST)
    sites_all = NS
    restricted = restricted.reshape(sites_all, NRHS, K3)
    onehot = (aggregate.reshape(sites_all)[:, None] == jnp.arange(NA, dtype=jnp.int32)[None, :]).astype(jnp.float32)
    coarse_rhs = jnp.einsum("sa,srk->akr", onehot, restricted, precision=lax.Precision.HIGHEST).reshape(NC3, NRHS)
    correction = jnp.dot(coarsest_inverse, coarse_rhs, precision=lax.Precision.HIGHEST,
                         preferred_element_type=jnp.float32).reshape(NA, K3, NRHS)
    per_site = jnp.einsum("sa,akr->skr", onehot, correction, precision=lax.Precision.HIGHEST)
    vectors = restrict.reshape(sites_all, K3, C)
    lifted = jnp.einsum("skc,skr->src", vectors, per_site, precision=lax.Precision.HIGHEST)
    solution = solution_gcr + lifted.reshape(solution_gcr.shape)
    return solution, residual
```

```python
import jax
import jax.numpy as jnp
from jax import lax
from jax.experimental import pallas as pl
from jax.experimental.pallas import tpu as pltpu
from jax.sharding import PartitionSpec as P

AXES = ("ta", "gz", "xy")
HIGHEST = lax.Precision.HIGHEST
F32 = jnp.float32
NT = (((1,), (1,)), ((), ()))
NN = (((1,), (0,)), ((), ()))


def dot(left, right, dims):
    return lax.dot_general(left, right, dims, precision=HIGHEST, preferred_element_type=F32)


def halo(field):
    sides = []
    for axis in AXES:
        count = lax.axis_size(axis)
        for step in (1, -1):
            sides.append(
                lax.ppermute(field, axis, [((i + step) % count, i) for i in range(count)])
            )
    return sides


def operator(field, sides, stencil, site):
    total = dot(field[site], stencil[site, 0], NT)
    for place, side in enumerate(sides):
        total = total + dot(side[site], stencil[site, 1 + place], NT)
    both = stencil[site, 7] + stencil[site, 8]
    return total + dot(field[1 - site], both, NT)


def first_kernel(field, s0, s1, s2, s3, s4, s5, stencil, image, differ):
    for site in range(2):
        value = operator(field, (s0, s1, s2, s3, s4, s5), stencil, site)
        image[site] = value
        differ[site] = field[site] - value


def second_kernel(
    label, differ, s0, s1, s2, s3, s4, s5, stencil, image, vectors, image_two, send
):
    rhs = differ.shape[1]
    lane = lax.broadcasted_iota(jnp.int32, (rhs, 128), 1)
    zero = jnp.zeros((32, 128), F32)
    packed = jnp.zeros((rhs, 128), F32)
    sums = [jnp.zeros((rhs, 1), F32) for _ in range(5)]
    for site in range(2):
        u, w = differ[site], image[site]
        q = operator(differ, (s0, s1, s2, s3, s4, s5), stencil, site)
        image_two[site] = q
        rows = vectors[site]
        packed = packed + dot(u, jnp.concatenate([rows, zero, zero, zero], axis=0), NT)
        packed = packed + dot(w, jnp.concatenate([zero, rows, zero, zero], axis=0), NT)
        packed = packed + dot(q, jnp.concatenate([zero, zero, rows, zero], axis=0), NT)
        for place, (one, other) in enumerate(((w, w), (w, u), (w, q), (q, u), (q, q))):
            sums[place] = sums[place] + jnp.sum(one * other, axis=1, keepdims=True)
    for place in range(5):
        packed = jnp.where(lane == 96 + place, sums[place], packed)
    packed = jnp.where(lane == 101, label[0].astype(F32), packed)
    for right in range(rhs):
        send[right] = jnp.broadcast_to(packed[right : right + 1, :], (16, 128))


def coarse_kernel(first_label, recv, inverse, send):
    lane = lax.broadcasted_iota(jnp.int32, (1, 128), 1)
    blocks = recv[...].reshape(4, 2, 4, 2, 8, 128)
    part = blocks[:, 0] + blocks[:, 1]
    part = part[:, :, 0] + part[:, :, 1]
    part = part.reshape(128, 128)
    total = jnp.sum(part, axis=0, keepdims=True)

    def pick(row, place):
        return jnp.sum(jnp.where(lane == place, row, 0.0), axis=1, keepdims=True)

    ww, wu, wq, qu, qq = [pick(total, 96 + place) for place in range(5)]
    first = wu / ww
    gamma = wq / ww
    sigma = (qu - gamma * wu) / (qq - gamma * wq)
    kappa = sigma * gamma - first
    labels = pick(part, 101) * 0.25
    mixed = part + kappa * pltpu.roll(part, 96, 1) - sigma * pltpu.roll(part, 64, 1)
    mixed = jnp.where(lane < 32, mixed, 0.0)
    mixed = mixed + pltpu.roll(mixed, 32, 1)
    mixed = mixed + pltpu.roll(mixed, 64, 1)
    group = (lane // 32).astype(F32)
    rows = []
    for place in range(16):
        chosen = labels == group + 4.0 * place
        rows.append(jnp.sum(jnp.where(chosen, mixed, 0.0), axis=0, keepdims=True))
    pieces = []
    for start in range(0, 256, 64):
        piece = inverse[start : start + 64, 0:128] * rows[0]
        for place in range(1, 16):
            piece = piece + inverse[start : start + 64, 128 * place : 128 * place + 128] * rows[place]
        pieces.append(piece)
    solved = jnp.concatenate(pieces, axis=0)
    halves = []
    for half in range(2):
        halves.append(
            jnp.sum(jnp.transpose(solved[128 * half : 128 * half + 128]), axis=0, keepdims=True)
        )
    scalars = jnp.where(lane == 32, sigma, jnp.where(lane == 33, kappa, 0.0))
    base = first_label[0].astype(F32)
    out = jnp.zeros((128, 128), F32)
    for place in range(8):
        row = halves[place // 4]
        if place % 4:
            row = pltpu.roll(row, 128 - 32 * (place % 4), 1)
        row = jnp.where(lane < 32, row, scalars)
        out = jnp.where(labels == base + float(place), row, out)
    out = out.reshape(4, 4, 8, 128)
    for t in range(8):
        for z in range(8):
            send[t, z] = out[t // 2, z // 2]


def last_kernel(recv, field, differ, image, image_two, vectors, solved, residual):
    got = jnp.concatenate(
        [
            jnp.sum(recv[t, z], axis=0, keepdims=True)
            for t in range(8)
            for z in range(0, 8, 2)
        ],
        axis=0,
    )
    correction = got[:, 0:32]
    sigma, kappa = got[:, 32:33], got[:, 33:34]
    for site in range(2):
        b, u, w, q = field[site], differ[site], image[site], image_two[site]
        residual[site] = u + kappa * w - sigma * q
        solved[site] = (1.0 - kappa) * b + sigma * u + dot(correction, vectors[site], NN)


def call(kernel, scalars, arrays, outs, name):
    shapes = [jax.ShapeDtypeStruct(shape, F32) for shape in outs]
    return pl.pallas_call(
        kernel,
        out_shape=shapes,
        in_specs=[pl.BlockSpec(memory_space=pltpu.SMEM)] * len(scalars)
        + [pl.BlockSpec(memory_space=pltpu.VMEM)] * len(arrays),
        out_specs=[pl.BlockSpec(memory_space=pltpu.VMEM)] * len(outs),
        compiler_params=pltpu.CompilerParams(vmem_limit_bytes=16 * 1024 * 1024),
        name=name,
    )(*scalars, *arrays)


def body(right_side, stencil, restrict, aggregate, coarsest_inverse):
    field = right_side[0, 0, 0]
    blocks = stencil[0, 0, 0]
    vectors = restrict[0, 0, 0]
    local = field.shape
    image, differ = call(
        first_kernel, (), (field, *halo(field), blocks), (local, local), "first_image"
    )
    image_two, send = call(
        second_kernel,
        (aggregate.reshape(2),),
        (differ, *halo(differ), blocks, image, vectors),
        (local, (32, 16, 128)),
        "second_image",
    )
    recv = lax.all_to_all(send.reshape(512, 128), AXES, 0, 0, tiled=True)
    first_label = (lax.axis_index("xy") * 8).astype(jnp.int32).reshape(1)
    (back,) = call(
        coarse_kernel,
        (first_label,),
        (recv.reshape(8, 8, 8, 128), coarsest_inverse),
        ((8, 8, 8, 128),),
        "coarse_solve",
    )
    home = lax.all_to_all(back.reshape(512, 128), AXES, 0, 0, tiled=True)
    solved, residual = call(
        last_kernel,
        (),
        (home.reshape(8, 8, 8, 128), field, differ, image, image_two, vectors),
        (local, local),
        "last_update",
    )
    return solved[None, None, None], residual[None, None, None]


def solution(mesh):
    return jax.shard_map(
        body,
        mesh=mesh,
        in_specs=(
            P("ta", "gz", "xy", None, None, None),
            P("ta", "gz", "xy", None, None, None, None),
            P("ta", "gz", "xy", None, None, None),
            P("ta", "gz", "xy", None),
            P("xy", None),
        ),
        out_specs=(P("ta", "gz", "xy", None, None, None), P("ta", "gz", "xy", None, None, None)),
        check_vma=False,
    )
```

```python
import jax
import jax.numpy as jnp
from jax import lax
from jax.experimental import pallas as pl
from jax.experimental.pallas import tpu as pltpu
from jax.sharding import Mesh
from jax.sharding import PartitionSpec as P

TA, GZ, XY = ("T", "a"), ("Z", "b"), ("Y", "c")
BLOCK = ("a", "b", "c")
LATTICE = ("T", "Z", "Y")
OUTER = [(1, 2), (2, 1), (3, 4), (4, 3), (5, 6), (6, 5), (7, 0), (0, 7)]
HIGHEST = lax.Precision.HIGHEST
F32 = jnp.float32
BF16 = jnp.bfloat16
NT = (((1,), (1,)), ((), ()))
NN = (((1,), (0,)), ((), ()))


def corner():
    a, b, c = (lax.axis_index(name) for name in BLOCK)
    return (4 * (1 - a) + 2 * b + c, 4 * a + 2 * (1 - b) + c, 4 * a + 2 * b + 1 - c)


def dot(left, right, dims):
    return lax.dot_general(left, right, dims, precision=HIGHEST, preferred_element_type=F32)


def split(value):
    high = value.astype(BF16)
    return high, (value - high.astype(F32)).astype(BF16)


def prepare_kernel(stencil, weights):
    a, b, c = (lax.axis_index(name) for name in BLOCK)
    order = (1 + a, 2 - a, 3 + b, 4 - b, 5 + c, 6 - c)
    rows = lax.broadcasted_iota(jnp.int32, (128, 128), 0)
    cols = lax.broadcasted_iota(jnp.int32, (128, 128), 1)
    unit = jnp.where(rows == cols, 1.0, 0.0).astype(F32)
    for site in range(2):
        for slot in range(8):
            if slot == 0:
                block = stencil[site, 0] - unit
            elif slot == 1:
                block = stencil[site, 7] + stencil[site, 8]
            else:
                block = stencil[site, order[slot - 2]]
            high, low = split(jnp.transpose(block))
            start = 128 * (slot % 2)
            weights[site, slot // 2, start : start + 128, 0:128] = high
            weights[site, slot // 2, start : start + 128, 128:256] = low


def change(place, field, near, outer, weights, site):
    sides = [field[site], field[1 - site]]
    for axis in range(3):
        sides.append(near[place[axis], site])
        sides.append(outer[axis][site])
    total = jnp.zeros((64, 256), F32)
    for pair in range(4):
        high, low = split(jnp.concatenate(sides[2 * pair : 2 * pair + 2], axis=1))
        both = jnp.concatenate([high, low], axis=0)
        total = total + lax.dot_general(
            both, weights[site, pair], NN, preferred_element_type=F32
        )
    half = total[0:32] + total[32:64]
    return half[:, 0:128] + half[:, 128:256]


def first_kernel(field, near, o0, o1, o2, weights, image, differ, send):
    place = corner()
    for site in range(2):
        value = change(place, field, near, (o0, o1, o2), weights, site)
        image[site] = field[site] + value
        differ[site] = -value
        for other in range(8):
            send[other, site] = -value


def padded(vectors, start):
    rows = jnp.concatenate([vectors[0], vectors[1]], axis=1)
    parts = [rows]
    if start:
        parts.insert(0, jnp.zeros((start, 256), F32))
    if start < 96:
        parts.append(jnp.zeros((96 - start, 256), F32))
    return jnp.concatenate(parts, axis=0)


def inner(one, other):
    return jnp.sum(one[0] * other[0] + one[1] * other[1], axis=1, keepdims=True)


def wide(field):
    return jnp.concatenate([field[0], field[1]], axis=1)


def early_kernel(label, differ, image, vectors, packed):
    lane = lax.broadcasted_iota(jnp.int32, (32, 128), 1)
    value = dot(wide(differ), padded(vectors, 0), NT)
    value = value + dot(wide(image), padded(vectors, 32), NT)
    value = jnp.where(lane == 96, inner(image, image), value)
    value = jnp.where(lane == 97, inner(image, differ), value)
    packed[...] = jnp.where(lane == 101, label[0].astype(F32), value)


def second_kernel(
    differ, near, o0, o1, o2, weights, image, vectors, early, image_two, send
):
    lane = lax.broadcasted_iota(jnp.int32, (32, 128), 1)
    values = []
    place = corner()
    for site in range(2):
        value = differ[site] + change(place, differ, near, (o0, o1, o2), weights, site)
        image_two[site] = value
        values.append(value)
    packed = early[...] + dot(wide(values), padded(vectors, 64), NT)
    packed = jnp.where(lane == 98, inner(image, values), packed)
    packed = jnp.where(lane == 99, inner(differ, values), packed)
    packed = jnp.where(lane == 100, inner(values, values), packed)
    for group in range(4):
        for c in range(2):
            send[2 * group + c] = packed[8 * group : 8 * group + 8]


def gather_kernel(recv, send):
    total = recv[0]
    for other in range(1, 8):
        total = total + recv[other]
    for right in range(8):
        send[right] = jnp.broadcast_to(total[right : right + 1], (8, 128))


def coarse_kernel(recv, inverse, send, rows_held, arrived):
    half = lax.rem(lax.axis_index("Z"), 2)
    copies = []
    for part in range(2):
        start = pl.multiple_of(128 * half + 64 * part, 64)
        copy = pltpu.make_async_copy(
            inverse.at[pl.ds(start, 64)], rows_held.at[pl.ds(64 * part, 64)], arrived.at[part]
        )
        copy.start()
        copies.append(copy)
    lane = lax.broadcasted_iota(jnp.int32, (1, 128), 1)
    part = recv[...]
    total = jnp.sum(part, axis=0, keepdims=True)

    def pick(row, place):
        return jnp.sum(jnp.where(lane == place, row, 0.0), axis=1, keepdims=True)

    ww, wu, wq, qu, qq = [pick(total, 96 + place) for place in range(5)]
    first = wu / ww
    gamma = wq / ww
    sigma = (qu - gamma * wu) / (qq - gamma * wq)
    kappa = sigma * gamma - first
    labels = pick(part, 101) * 0.125
    mixed = part + kappa * pltpu.roll(part, 96, 1) - sigma * pltpu.roll(part, 64, 1)
    mixed = jnp.where(lane < 32, mixed, 0.0)
    mixed = mixed + pltpu.roll(mixed, 32, 1)
    mixed = mixed + pltpu.roll(mixed, 64, 1)
    group = (lane // 32).astype(F32)
    rows = []
    for place in range(16):
        chosen = labels == group + 4.0 * place
        rows.append(jnp.sum(jnp.where(chosen, mixed, 0.0), axis=0, keepdims=True))
    pieces = []
    for part in range(2):
        copies[part].wait()
        begin = 64 * part
        piece = rows_held[begin : begin + 64, 0:128] * rows[0]
        for place in range(1, 16):
            piece = piece + rows_held[begin : begin + 64, 128 * place : 128 * place + 128] * rows[place]
        pieces.append(piece)
    solved = jnp.transpose(jnp.concatenate(pieces, axis=0))
    solved = jnp.sum(solved, axis=0, keepdims=True)
    scalars = jnp.where(lane == 32, sigma, jnp.where(lane == 33, kappa, 0.0))
    base = (8 * lax.axis_index(XY) + 4 * half).astype(F32)
    out = jnp.zeros((64, 128), F32)
    for place in range(4):
        row = pltpu.roll(solved, 128 - 32 * place, 1) if place else solved
        row = jnp.where(lane < 32, row, scalars)
        out = jnp.where(labels == base + float(place), row, out)
    send[...] = out


def spread_kernel(recv, send):
    rows = []
    for right in range(8):
        rows.append(jnp.sum(recv[8 * right : 8 * right + 8], axis=0, keepdims=True))
    value = jnp.concatenate(rows, axis=0)
    for other in range(8):
        send[other] = value


def last_kernel(recv, field, differ, image, image_two, vectors, solved, residual):
    got = jnp.concatenate([recv[2 * group] + recv[2 * group + 1] for group in range(4)], axis=0)
    correction = got[:, 0:32]
    sigma, kappa = got[:, 32:33], got[:, 33:34]
    for site in range(2):
        b, u, w, q = field[site], differ[site], image[site], image_two[site]
        residual[site] = u + kappa * w - sigma * q
        solved[site] = (1.0 - kappa) * b + sigma * u + dot(correction, vectors[site], NN)


def call(kernel, scalars, arrays, outs, name, cost=None):
    return pl.pallas_call(
        kernel,
        out_shape=[jax.ShapeDtypeStruct(shape, kind) for shape, kind in outs],
        in_specs=[pl.BlockSpec(memory_space=pltpu.SMEM)] * len(scalars)
        + [pl.BlockSpec(memory_space=pltpu.VMEM)] * len(arrays),
        out_specs=[pl.BlockSpec(memory_space=pltpu.VMEM)] * len(outs),
        compiler_params=pltpu.CompilerParams(vmem_limit_bytes=16 * 1024 * 1024),
        cost_estimate=cost,
        name=name,
    )(*scalars, *arrays)


def exchange(field, copies):
    outer = [lax.ppermute(field, axis, OUTER) for axis in (TA, XY, GZ)]
    near = lax.all_to_all(copies, BLOCK, 0, 0, tiled=True)
    return near.reshape(8, *field.shape), outer[0], outer[2], outer[1]


def body(right_side, stencil, restrict, aggregate, coarsest_inverse):
    field = right_side[0, 0, 0]
    vectors = restrict[0, 0, 0]
    local = (field.shape, F32)
    label = aggregate.reshape(2)
    (weights,) = call(
        prepare_kernel,
        (),
        (stencil[0, 0, 0],),
        (((2, 4, 256, 256), BF16),),
        "prepare",
        pl.CostEstimate(flops=1 << 20, bytes_accessed=1 << 23, transcendentals=0),
    )
    copies = jnp.broadcast_to(field[None], (8, *field.shape))
    image, differ, copies = call(
        first_kernel,
        (),
        (field, *exchange(field, copies), weights),
        (local, local, ((8, *field.shape), F32)),
        "first_image",
    )
    (early,) = call(
        early_kernel, (label,), (differ, image, vectors), (((32, 128), F32),), "early_part"
    )
    image_two, send = call(
        second_kernel,
        (),
        (differ, *exchange(differ, copies), weights, image, vectors, early),
        (local, ((8, 8, 128), F32)),
        "second_image",
    )
    recv = lax.all_to_all(send, BLOCK, 0, 0, tiled=True)
    (send,) = call(gather_kernel, (), (recv,), (((8, 8, 128), F32),), "block_sum")
    recv = lax.all_to_all(send.reshape(64, 128), LATTICE, 0, 0, tiled=True)
    send = pl.pallas_call(
        coarse_kernel,
        out_shape=jax.ShapeDtypeStruct((64, 128), F32),
        in_specs=[pl.BlockSpec(memory_space=pltpu.VMEM), pl.BlockSpec(memory_space=pltpu.HBM)],
        out_specs=pl.BlockSpec(memory_space=pltpu.VMEM),
        scratch_shapes=[pltpu.VMEM((128, 2048), F32), pltpu.SemaphoreType.DMA((2,))],
        compiler_params=pltpu.CompilerParams(vmem_limit_bytes=65900000),
        name="coarse_solve",
    )(recv, coarsest_inverse)
    recv = lax.all_to_all(send, LATTICE, 0, 0, tiled=True)
    (send,) = call(spread_kernel, (), (recv,), (((8, 8, 128), F32),), "block_spread")
    recv = lax.all_to_all(send, BLOCK, 0, 0, tiled=True)
    solved, residual = call(
        last_kernel,
        (),
        (recv, field, differ, image, image_two, vectors),
        (local, local),
        "last_update",
    )
    return solved[None, None, None], residual[None, None, None]


def solution(mesh):
    blocks = Mesh(mesh.devices.reshape(4, 2, 4, 2, 4, 2), ("T", "a", "Z", "b", "Y", "c"))
    spec = P(TA, GZ, XY)
    return jax.shard_map(
        body,
        mesh=blocks,
        in_specs=(spec, spec, spec, spec, P(XY)),
        out_specs=(spec, spec),
        check_vma=False,
    )
```

```python
import jax
import jax.numpy as jnp
from jax import lax
from jax.experimental import pallas as pl
from jax.experimental.pallas import tpu as pltpu
from jax.sharding import Mesh
from jax.sharding import PartitionSpec as P

TA, GZ, XY = ("T", "a"), ("Z", "b"), ("Y", "c")
BLOCK = ("a", "b", "c")
LATTICE = ("T", "Z", "Y")
OUTER = [(1, 2), (2, 1), (3, 4), (4, 3), (5, 6), (6, 5), (7, 0), (0, 7)]
HIGHEST = lax.Precision.HIGHEST
F32 = jnp.float32
BF16 = jnp.bfloat16
NT = (((1,), (1,)), ((), ()))
NN = (((1,), (0,)), ((), ()))


def corner():
    a, b, c = (lax.axis_index(name) for name in BLOCK)
    return (4 * (1 - a) + 2 * b + c, 4 * a + 2 * (1 - b) + c, 4 * a + 2 * b + 1 - c)


def dot(left, right, dims):
    return lax.dot_general(left, right, dims, precision=HIGHEST, preferred_element_type=F32)


def split(value):
    high = value.astype(BF16)
    return high, (value - high.astype(F32)).astype(BF16)


def prepare_kernel(stencil, weights):
    a, b, c = (lax.axis_index(name) for name in BLOCK)
    order = (1 + a, 2 - a, 3 + b, 4 - b, 5 + c, 6 - c)
    rows = lax.broadcasted_iota(jnp.int32, (128, 128), 0)
    cols = lax.broadcasted_iota(jnp.int32, (128, 128), 1)
    unit = jnp.where(rows == cols, 1.0, 0.0).astype(F32)
    for site in range(2):
        for slot in range(8):
            if slot == 0:
                block = stencil[site, 0] - unit
            elif slot == 1:
                block = stencil[site, 7] + stencil[site, 8]
            else:
                block = stencil[site, order[slot - 2]]
            high, low = split(jnp.transpose(block))
            start = 128 * (slot % 2)
            weights[site, slot // 2, start : start + 128, 0:128] = high
            weights[site, slot // 2, start : start + 128, 128:256] = low


def change(place, field, near, outer, weights, site):
    sides = [field[site], field[1 - site]]
    for axis in range(3):
        sides.append(near[place[axis], site])
        sides.append(outer[axis][site])
    total = jnp.zeros((64, 256), F32)
    for pair in range(4):
        high, low = split(jnp.concatenate(sides[2 * pair : 2 * pair + 2], axis=1))
        both = jnp.concatenate([high, low], axis=0)
        total = total + lax.dot_general(
            both, weights[site, pair], NN, preferred_element_type=F32
        )
    half = total[0:32] + total[32:64]
    return half[:, 0:128] + half[:, 128:256]


def first_kernel(field, near, o0, o1, o2, weights, image, differ, send):
    place = corner()
    for site in range(2):
        value = change(place, field, near, (o0, o1, o2), weights, site)
        image[site] = field[site] + value
        differ[site] = -value
        for other in range(8):
            send[other, site] = -value


def padded(vectors, start):
    rows = jnp.concatenate([vectors[0], vectors[1]], axis=1)
    parts = [rows]
    if start:
        parts.insert(0, jnp.zeros((start, 256), F32))
    if start < 96:
        parts.append(jnp.zeros((96 - start, 256), F32))
    return jnp.concatenate(parts, axis=0)


def inner(one, other):
    return jnp.sum(one[0] * other[0] + one[1] * other[1], axis=1, keepdims=True)


def wide(field):
    return jnp.concatenate([field[0], field[1]], axis=1)


def early_kernel(label, differ, image, vectors, packed):
    lane = lax.broadcasted_iota(jnp.int32, (32, 128), 1)
    value = dot(wide(differ), padded(vectors, 0), NT)
    value = value + dot(wide(image), padded(vectors, 32), NT)
    value = jnp.where(lane == 96, inner(image, image), value)
    value = jnp.where(lane == 97, inner(image, differ), value)
    packed[...] = jnp.where(lane == 101, label[0].astype(F32), value)


def second_kernel(
    differ, near, o0, o1, o2, weights, image, vectors, early, image_two, send
):
    lane = lax.broadcasted_iota(jnp.int32, (32, 128), 1)
    values = []
    place = corner()
    for site in range(2):
        value = differ[site] + change(place, differ, near, (o0, o1, o2), weights, site)
        image_two[site] = value
        values.append(value)
    packed = early[...] + dot(wide(values), padded(vectors, 64), NT)
    packed = jnp.where(lane == 98, inner(image, values), packed)
    packed = jnp.where(lane == 99, inner(differ, values), packed)
    packed = jnp.where(lane == 100, inner(values, values), packed)
    for group in range(4):
        for c in range(2):
            send[2 * group + c] = packed[8 * group : 8 * group + 8]


def copy_kernel(field, send):
    for other in range(8):
        send[other] = field[...]


def gather_kernel(recv, send):
    total = recv[0]
    for other in range(1, 8):
        total = total + recv[other]
    for other in range(64):
        send[other] = total


def coarse_kernel(recv, inverse, send, rows_held, arrived):
    copies = []
    for part in range(2):
        copy = pltpu.make_async_copy(
            inverse.at[pl.ds(128 * part, 128)], rows_held.at[pl.ds(128 * part, 128)], arrived.at[part]
        )
        copy.start()
        copies.append(copy)
    lane = lax.broadcasted_iota(jnp.int32, (8, 128), 1)

    def pick(row, place):
        return jnp.sum(jnp.where(lane == place, row, 0.0), axis=1, keepdims=True)

    total = recv[0]
    for source in range(1, 64):
        total = total + recv[source]
    ww, wu, wq, qu, qq = [pick(total, 96 + place) for place in range(5)]
    first = wu / ww
    gamma = wq / ww
    sigma = (qu - gamma * wu) / (qq - gamma * wq)
    kappa = sigma * gamma - first
    group = (lane // 32).astype(F32)
    rows = [jnp.zeros((8, 128), F32) for _ in range(16)]
    for source in range(64):
        part = recv[source]
        code = pick(part, 101) * 0.125 - group
        mixed = part + kappa * pltpu.roll(part, 96, 1) - sigma * pltpu.roll(part, 64, 1)
        mixed = jnp.where(lane < 32, mixed, 0.0)
        mixed = mixed + pltpu.roll(mixed, 32, 1)
        mixed = mixed + pltpu.roll(mixed, 64, 1)
        for place in range(16):
            rows[place] = rows[place] + jnp.where(code == 4.0 * place, mixed, 0.0)
    high, low = split(jnp.concatenate(rows, axis=1))
    both = jnp.concatenate([high, low], axis=0)
    base = (8 * lax.axis_index(XY)).astype(F32)
    own = 16 * lax.axis_index("T") + 4 * lax.axis_index("Z")
    labels = [pick(recv[own + y], 101) * 0.125 - base for y in range(4)]
    scalars = jnp.where(lane == 32, sigma, jnp.where(lane == 33, kappa, 0.0))
    out = [jnp.zeros((8, 128), F32) for _ in range(4)]
    for part in range(2):
        copies[part].wait()
        held_high, held_low = split(rows_held[128 * part : 128 * part + 128])
        value = lax.dot_general(both, held_high, NT, preferred_element_type=F32)
        value = value[0:8] + value[8:16]
        value = value + lax.dot_general(high, held_low, NT, preferred_element_type=F32)
        for place in range(4):
            row = pltpu.roll(value, 128 - 32 * place, 1) if place else value
            row = jnp.where(lane < 32, row, scalars)
            for y in range(4):
                out[y] = jnp.where(labels[y] == float(4 * part + place), row, out[y])
    for side in range(4):
        for y in range(4):
            for c in range(2):
                send[8 * side + 2 * y + c] = out[y]


def last_kernel(recv, field, differ, image, image_two, vectors, solved, residual):
    groups = []
    for group in range(4):
        total = recv[8 * group]
        for other in range(1, 8):
            total = total + recv[8 * group + other]
        groups.append(total)
    got = jnp.concatenate(groups, axis=0)
    correction = got[:, 0:32]
    sigma, kappa = got[:, 32:33], got[:, 33:34]
    for site in range(2):
        b, u, w, q = field[site], differ[site], image[site], image_two[site]
        residual[site] = u + kappa * w - sigma * q
        solved[site] = (1.0 - kappa) * b + sigma * u + dot(correction, vectors[site], NN)


def call(kernel, scalars, arrays, outs, name, cost=None):
    return pl.pallas_call(
        kernel,
        out_shape=[jax.ShapeDtypeStruct(shape, kind) for shape, kind in outs],
        in_specs=[pl.BlockSpec(memory_space=pltpu.SMEM)] * len(scalars)
        + [pl.BlockSpec(memory_space=pltpu.VMEM)] * len(arrays),
        out_specs=[pl.BlockSpec(memory_space=pltpu.VMEM)] * len(outs),
        compiler_params=pltpu.CompilerParams(vmem_limit_bytes=16 * 1024 * 1024),
        cost_estimate=cost,
        name=name,
    )(*scalars, *arrays)


def exchange(field, copies):
    outer = [lax.ppermute(field, axis, OUTER) for axis in (TA, XY, GZ)]
    near = lax.all_to_all(copies, BLOCK, 0, 0, tiled=True)
    return near.reshape(8, *field.shape), outer[0], outer[2], outer[1]


def body(right_side, stencil, restrict, aggregate, coarsest_inverse):
    field = right_side[0, 0, 0]
    vectors = restrict[0, 0, 0]
    local = (field.shape, F32)
    label = aggregate.reshape(2)
    (weights,) = call(
        prepare_kernel,
        (),
        (stencil[0, 0, 0],),
        (((2, 4, 256, 256), BF16),),
        "prepare",
        pl.CostEstimate(flops=1 << 20, bytes_accessed=1 << 23, transcendentals=0),
    )
    (copies,) = call(copy_kernel, (), (field,), (((8, *field.shape), F32),), "copies")
    image, differ, copies = call(
        first_kernel,
        (),
        (field, *exchange(field, copies), weights),
        (local, local, ((8, *field.shape), F32)),
        "first_image",
    )
    (early,) = call(
        early_kernel, (label,), (differ, image, vectors), (((32, 128), F32),), "early_part"
    )
    image_two, send = call(
        second_kernel,
        (),
        (differ, *exchange(differ, copies), weights, image, vectors, early),
        (local, ((8, 8, 128), F32)),
        "second_image",
    )
    recv = lax.all_to_all(send, BLOCK, 0, 0, tiled=True)
    (send,) = call(gather_kernel, (), (recv,), (((64, 8, 128), F32),), "block_sum")
    recv = lax.all_to_all(send, LATTICE, 0, 0, tiled=True)
    send = pl.pallas_call(
        coarse_kernel,
        out_shape=jax.ShapeDtypeStruct((32, 8, 128), F32),
        in_specs=[pl.BlockSpec(memory_space=pltpu.VMEM), pl.BlockSpec(memory_space=pltpu.HBM)],
        out_specs=pl.BlockSpec(memory_space=pltpu.VMEM),
        scratch_shapes=[pltpu.VMEM((256, 2048), F32), pltpu.SemaphoreType.DMA((2,))],
        compiler_params=pltpu.CompilerParams(vmem_limit_bytes=65100000),
        name="coarse_solve",
    )(recv, coarsest_inverse)
    recv = lax.all_to_all(send, ("a", "b", "Y", "c"), 0, 0, tiled=True)
    solved, residual = call(
        last_kernel,
        (),
        (recv, field, differ, image, image_two, vectors),
        (local, local),
        "last_update",
    )
    return solved[None, None, None], residual[None, None, None]


def solution(mesh):
    blocks = Mesh(mesh.devices.reshape(4, 2, 4, 2, 4, 2), ("T", "a", "Z", "b", "Y", "c"))
    spec = P(TA, GZ, XY)
    return jax.shard_map(
        body,
        mesh=blocks,
        in_specs=(spec, spec, spec, spec, P(XY)),
        out_specs=(spec, spec),
        check_vma=False,
    )
```

```python
import jax
import jax.numpy as jnp
from jax import lax
from jax.experimental import pallas as pl
from jax.experimental.pallas import tpu as pltpu
from jax.sharding import Mesh
from jax.sharding import PartitionSpec as P


TA, GZ, XY = ("T", "a"), ("Z", "b"), ("Y", "c")
BLOCK = ("a", "b", "c")
LATTICE = ("T", "Z", "Y")
HIGHEST = lax.Precision.HIGHEST
F32 = jnp.float32
BF16 = jnp.bfloat16
NT = (((1,), (1,)), ((), ()))
NN = (((1,), (0,)), ((), ()))


def dot(left, right, dims):
    return lax.dot_general(left, right, dims, precision=HIGHEST, preferred_element_type=F32)


def split(value):
    high = value.astype(BF16)
    return high, (value - high.astype(F32)).astype(BF16)


def prepare_kernel(stencil, weights):
    rows = lax.broadcasted_iota(jnp.int32, (128, 128), 0)
    cols = lax.broadcasted_iota(jnp.int32, (128, 128), 1)
    unit = jnp.where(rows == cols, 1.0, 0.0).astype(F32)
    for site in range(2):
        for slot in range(8):
            if slot == 0:
                block = stencil[site, 0] - unit
            elif slot == 1:
                block = stencil[site, 7] + stencil[site, 8]
            else:
                block = stencil[site, slot - 1]
            high, low = split(jnp.transpose(block))
            start = 128 * (slot % 2)
            weights[site, slot // 2, start : start + 128, 0:128] = high
            weights[site, slot // 2, start : start + 128, 128:256] = low


def change(field, sides, weights, site):
    sides = [field[site], field[1 - site]] + [side[site] for side in sides]
    total = jnp.zeros((64, 256), F32)
    for pair in range(4):
        high, low = split(jnp.concatenate(sides[2 * pair : 2 * pair + 2], axis=1))
        both = jnp.concatenate([high, low], axis=0)
        total = total + lax.dot_general(
            both, weights[site, pair], NN, preferred_element_type=F32
        )
    half = total[0:32] + total[32:64]
    return half[:, 0:128] + half[:, 128:256]


def first_kernel(field, s0, s1, s2, s3, s4, s5, weights, image, differ):
    for site in range(2):
        value = change(field, (s0, s1, s2, s3, s4, s5), weights, site)
        image[site] = field[site] + value
        differ[site] = -value


def padded(vectors, start):
    rows = jnp.concatenate([vectors[0], vectors[1]], axis=1)
    parts = [rows]
    if start:
        parts.insert(0, jnp.zeros((start, 256), F32))
    if start < 96:
        parts.append(jnp.zeros((96 - start, 256), F32))
    return jnp.concatenate(parts, axis=0)


def inner(one, other):
    return jnp.sum(one[0] * other[0] + one[1] * other[1], axis=1, keepdims=True)


def wide(field):
    return jnp.concatenate([field[0], field[1]], axis=1)


def early_kernel(label, differ, image, vectors, packed):
    lane = lax.broadcasted_iota(jnp.int32, (32, 128), 1)
    value = dot(wide(differ), padded(vectors, 0), NT)
    value = value + dot(wide(image), padded(vectors, 32), NT)
    value = jnp.where(lane == 96, inner(image, image), value)
    value = jnp.where(lane == 97, inner(image, differ), value)
    packed[...] = jnp.where(lane == 101, label[0].astype(F32), value)


def second_kernel(
    differ, s0, s1, s2, s3, s4, s5, weights, image, vectors, early, image_two, send
):
    lane = lax.broadcasted_iota(jnp.int32, (32, 128), 1)
    values = []
    for site in range(2):
        value = differ[site] + change(differ, (s0, s1, s2, s3, s4, s5), weights, site)
        image_two[site] = value
        values.append(value)
    packed = early[...] + dot(wide(values), padded(vectors, 64), NT)
    packed = jnp.where(lane == 98, inner(image, values), packed)
    packed = jnp.where(lane == 99, inner(differ, values), packed)
    packed = jnp.where(lane == 100, inner(values, values), packed)
    for group in range(4):
        for c in range(2):
            send[2 * group + c] = packed[8 * group : 8 * group + 8]


def gather_kernel(recv, send):
    total = recv[0]
    for other in range(1, 8):
        total = total + recv[other]
    for other in range(64):
        send[other] = total


def coarse_kernel(recv, inverse, send):
    lane = lax.broadcasted_iota(jnp.int32, (8, 128), 1)

    def pick(row, place):
        return jnp.sum(jnp.where(lane == place, row, 0.0), axis=1, keepdims=True)

    total = recv[0]
    for source in range(1, 64):
        total = total + recv[source]
    ww, wu, wq, qu, qq = [pick(total, 96 + place) for place in range(5)]
    first = wu / ww
    gamma = wq / ww
    sigma = (qu - gamma * wu) / (qq - gamma * wq)
    kappa = sigma * gamma - first
    group = (lane // 32).astype(F32)
    rows = [jnp.zeros((8, 128), F32) for _ in range(16)]
    for source in range(64):
        part = recv[source]
        code = pick(part, 101) * 0.125 - group
        mixed = part + kappa * pltpu.roll(part, 96, 1) - sigma * pltpu.roll(part, 64, 1)
        mixed = jnp.where(lane < 32, mixed, 0.0)
        mixed = mixed + pltpu.roll(mixed, 32, 1)
        mixed = mixed + pltpu.roll(mixed, 64, 1)
        for place in range(16):
            rows[place] = rows[place] + jnp.where(code == 4.0 * place, mixed, 0.0)
    high, low = split(jnp.concatenate(rows, axis=1))
    both = jnp.concatenate([high, low], axis=0)
    base = (8 * lax.axis_index(XY)).astype(F32)
    own = 16 * lax.axis_index("T") + 4 * lax.axis_index("Z")
    labels = [pick(recv[own + y], 101) * 0.125 - base for y in range(4)]
    scalars = jnp.where(lane == 32, sigma, jnp.where(lane == 33, kappa, 0.0))
    out = [jnp.zeros((8, 128), F32) for _ in range(4)]
    for part in range(2):
        held_high, held_low = split(inverse[128 * part : 128 * part + 128])
        value = lax.dot_general(both, held_high, NT, preferred_element_type=F32)
        value = value[0:8] + value[8:16]
        value = value + lax.dot_general(high, held_low, NT, preferred_element_type=F32)
        for place in range(4):
            row = pltpu.roll(value, 128 - 32 * place, 1) if place else value
            row = jnp.where(lane < 32, row, scalars)
            for y in range(4):
                out[y] = jnp.where(labels[y] == float(4 * part + place), row, out[y])
    for side in range(4):
        for y in range(4):
            for c in range(2):
                send[8 * side + 2 * y + c] = out[y]


def last_kernel(recv, field, differ, image, image_two, vectors, solved, residual):
    groups = []
    for group in range(4):
        total = recv[8 * group]
        for other in range(1, 8):
            total = total + recv[8 * group + other]
        groups.append(total)
    got = jnp.concatenate(groups, axis=0)
    correction = got[:, 0:32]
    sigma, kappa = got[:, 32:33], got[:, 33:34]
    for site in range(2):
        b, u, w, q = field[site], differ[site], image[site], image_two[site]
        residual[site] = u + kappa * w - sigma * q
        solved[site] = (1.0 - kappa) * b + sigma * u + dot(correction, vectors[site], NN)


def call(kernel, scalars, arrays, outs, name, cost=None):
    return pl.pallas_call(
        kernel,
        out_shape=[jax.ShapeDtypeStruct(shape, kind) for shape, kind in outs],
        in_specs=[pl.BlockSpec(memory_space=pltpu.SMEM)] * len(scalars)
        + [pl.BlockSpec(memory_space=pltpu.VMEM)] * len(arrays),
        out_specs=[pl.BlockSpec(memory_space=pltpu.VMEM)] * len(outs),
        compiler_params=pltpu.CompilerParams(vmem_limit_bytes=16 * 1024 * 1024),
        cost_estimate=cost,
        name=name,
    )(*scalars, *arrays)


def halo(field):
    sides = []
    for axis in (TA, GZ, XY):
        for step in (1, -1):
            sides.append(lax.ppermute(field, axis, [((i + step) % 8, i) for i in range(8)]))
    return sides


def body(right_side, stencil, restrict, aggregate, coarsest_inverse):
    field = right_side[0, 0, 0]
    vectors = restrict[0, 0, 0]
    local = (field.shape, F32)
    label = aggregate.reshape(2)
    (weights,) = call(
        prepare_kernel,
        (),
        (stencil[0, 0, 0],),
        (((2, 4, 256, 256), BF16),),
        "prepare",
        pl.CostEstimate(flops=1 << 20, bytes_accessed=1 << 23, transcendentals=0),
    )
    image, differ = call(
        first_kernel,
        (),
        (field, *halo(field), weights),
        (local, local),
        "first_image",
    )
    (early,) = call(
        early_kernel, (label,), (differ, image, vectors), (((32, 128), F32),), "early_part"
    )
    image_two, send = call(
        second_kernel,
        (),
        (differ, *halo(differ), weights, image, vectors, early),
        (local, ((8, 8, 128), F32)),
        "second_image",
    )
    recv = lax.all_to_all(send, BLOCK, 0, 0, tiled=True)
    (send,) = call(gather_kernel, (), (recv,), (((64, 8, 128), F32),), "block_sum")
    recv = lax.all_to_all(send, LATTICE, 0, 0, tiled=True)
    (send,) = call(
        coarse_kernel, (), (recv, coarsest_inverse), (((32, 8, 128), F32),), "coarse_solve"
    )
    recv = lax.all_to_all(send, ("a", "b", "Y", "c"), 0, 0, tiled=True)
    solved, residual = call(
        last_kernel,
        (),
        (recv, field, differ, image, image_two, vectors),
        (local, local),
        "last_update",
    )
    return solved[None, None, None], residual[None, None, None]


def solution(mesh):
    blocks = Mesh(mesh.devices.reshape(4, 2, 4, 2, 4, 2), ("T", "a", "Z", "b", "Y", "c"))
    spec = P(TA, GZ, XY)
    return jax.shard_map(
        body,
        mesh=blocks,
        in_specs=(spec, spec, spec, spec, P(XY)),
        out_specs=(spec, spec),
        check_vma=False,
    )
```

```python
import jax
import jax.numpy as jnp
from jax import lax
from jax.experimental import pallas as pl
from jax.experimental.pallas import tpu as pltpu
from jax.sharding import Mesh
from jax.sharding import PartitionSpec as P


TA, GZ, XY = ("T", "a"), ("Z", "b"), ("Y", "c")
BLOCK = ("a", "b", "c")
LATTICE = ("T", "Z", "Y")
SIDES = [(GZ, 1), (TA, 1), (XY, 1), (GZ, -1), (TA, -1), (XY, -1)]
OFFSETS = [3, 1, 5, 4, 2, 6]
HIGHEST = lax.Precision.HIGHEST
F32 = jnp.float32
BF16 = jnp.bfloat16
NT = (((1,), (1,)), ((), ()))
NN = (((1,), (0,)), ((), ()))


def dot(left, right, dims):
    return lax.dot_general(left, right, dims, precision=HIGHEST, preferred_element_type=F32)


def split(value):
    high = value.astype(BF16)
    return high, (value - high.astype(F32)).astype(BF16)


def prepare_kernel(stencil, weights):
    rows = lax.broadcasted_iota(jnp.int32, (128, 128), 0)
    cols = lax.broadcasted_iota(jnp.int32, (128, 128), 1)
    unit = jnp.where(rows == cols, 1.0, 0.0).astype(F32)
    for site in range(2):
        for slot in range(8):
            if slot == 0:
                block = stencil[site, 0] - unit
            elif slot == 1:
                block = stencil[site, 7] + stencil[site, 8]
            else:
                block = stencil[site, OFFSETS[slot - 2]]
            high, low = split(jnp.transpose(block))
            start = 128 * (slot % 2)
            weights[site, slot // 2, start : start + 128, 0:128] = high
            weights[site, slot // 2, start : start + 128, 128:256] = low


def change(field, sides, weights, site):
    sides = [field[site], field[1 - site]] + [side[site] for side in sides]
    total = jnp.zeros((64, 256), F32)
    for pair in range(4):
        high, low = split(jnp.concatenate(sides[2 * pair : 2 * pair + 2], axis=1))
        both = jnp.concatenate([high, low], axis=0)
        total = total + lax.dot_general(
            both, weights[site, pair], NN, preferred_element_type=F32
        )
    half = total[0:32] + total[32:64]
    return half[:, 0:128] + half[:, 128:256]


def first_kernel(field, s0, s1, s2, s3, s4, s5, weights, image, differ):
    for site in range(2):
        value = change(field, (s0, s1, s2, s3, s4, s5), weights, site)
        image[site] = field[site] + value
        differ[site] = -value


def padded(vectors, start):
    rows = jnp.concatenate([vectors[0], vectors[1]], axis=1)
    parts = [rows]
    if start:
        parts.insert(0, jnp.zeros((start, 256), F32))
    if start < 96:
        parts.append(jnp.zeros((96 - start, 256), F32))
    return jnp.concatenate(parts, axis=0)


def inner(one, other):
    return jnp.sum(one[0] * other[0] + one[1] * other[1], axis=1, keepdims=True)


def wide(field):
    return jnp.concatenate([field[0], field[1]], axis=1)


def early_kernel(label, differ, image, vectors, inverse, packed, inverse_high, inverse_low):
    lane = lax.broadcasted_iota(jnp.int32, (32, 128), 1)
    value = dot(wide(differ), padded(vectors, 0), NT)
    value = value + dot(wide(image), padded(vectors, 32), NT)
    value = jnp.where(lane == 96, inner(image, image), value)
    value = jnp.where(lane == 97, inner(image, differ), value)
    packed[...] = jnp.where(lane == 101, label[0].astype(F32), value)
    for place in range(16):
        start = 128 * place
        high, low = split(jnp.transpose(inverse[:, start : start + 128]))
        inverse_high[start : start + 128] = high
        inverse_low[start : start + 128] = low


def second_kernel(
    differ, s0, s1, s2, s3, s4, s5, weights, image, vectors, early, image_two, send
):
    lane = lax.broadcasted_iota(jnp.int32, (32, 128), 1)
    values = []
    for site in range(2):
        value = differ[site] + change(differ, (s0, s1, s2, s3, s4, s5), weights, site)
        image_two[site] = value
        values.append(value)
    packed = early[...] + dot(wide(values), padded(vectors, 64), NT)
    packed = jnp.where(lane == 98, inner(image, values), packed)
    packed = jnp.where(lane == 99, inner(differ, values), packed)
    packed = jnp.where(lane == 100, inner(values, values), packed)
    for group in range(4):
        for c in range(2):
            send[2 * group + c] = packed[8 * group : 8 * group + 8]


def gather_kernel(recv, send):
    total = recv[0]
    for other in range(1, 8):
        total = total + recv[other]
    for other in range(64):
        send[other] = total


def coarse_kernel(recv, inverse_high, inverse_low, send, tiles, codes):
    lane = lax.broadcasted_iota(jnp.int32, (8, 128), 1)

    def pick(row, place):
        return jnp.sum(jnp.where(lane == place, row, 0.0), axis=1, keepdims=True)

    total = recv[0]
    for source in range(1, 64):
        total = total + recv[source]
    ww, wu, wq, qu, qq = [pick(total, 96 + place) for place in range(5)]
    first = wu / ww
    gamma = wq / ww
    sigma = (qu - gamma * wu) / (qq - gamma * wq)
    kappa = sigma * gamma - first
    group = (lane // 32).astype(F32)
    for source in range(64):
        part = recv[source]
        codes[source] = pick(part, 101) * 0.125 - group
        mixed = part + kappa * pltpu.roll(part, 96, 1) - sigma * pltpu.roll(part, 64, 1)
        mixed = jnp.where(lane < 32, mixed, 0.0)
        mixed = mixed + pltpu.roll(mixed, 32, 1)
        tiles[source] = mixed + pltpu.roll(mixed, 64, 1)
    rows = []
    for start in range(0, 16, 8):
        sums = [jnp.zeros((8, 128), F32) for _ in range(8)]
        for source in range(64):
            tile, code = tiles[source], codes[source]
            for place in range(8):
                sums[place] = sums[place] + jnp.where(code == 4.0 * (start + place), tile, 0.0)
        rows.extend(sums)
    high, low = split(jnp.concatenate(rows, axis=1))
    both = jnp.concatenate([high, low], axis=0)
    base = (8 * lax.axis_index(XY)).astype(F32)
    own = 16 * lax.axis_index("T") + 4 * lax.axis_index("Z")
    labels = [pick(recv[own + y], 101) * 0.125 - base for y in range(4)]
    scalars = jnp.where(lane == 32, sigma, jnp.where(lane == 33, kappa, 0.0))
    out = [jnp.zeros((8, 128), F32) for _ in range(4)]
    values = lax.dot_general(both, inverse_high[...], NN, preferred_element_type=F32)
    values = values[0:8] + values[8:16]
    values = values + lax.dot_general(high, inverse_low[...], NN, preferred_element_type=F32)
    for part in range(2):
        value = values[:, 128 * part : 128 * part + 128]
        for place in range(4):
            row = pltpu.roll(value, 128 - 32 * place, 1) if place else value
            row = jnp.where(lane < 32, row, scalars)
            for y in range(4):
                out[y] = jnp.where(labels[y] == float(4 * part + place), row, out[y])
    for side in range(4):
        for y in range(4):
            for c in range(2):
                send[8 * side + 2 * y + c] = out[y]


def last_kernel(recv, field, differ, image, image_two, vectors, solved, residual):
    groups = []
    for group in range(4):
        total = recv[8 * group]
        for other in range(1, 8):
            total = total + recv[8 * group + other]
        groups.append(total)
    got = jnp.concatenate(groups, axis=0)
    correction = got[:, 0:32]
    sigma, kappa = got[:, 32:33], got[:, 33:34]
    for site in range(2):
        b, u, w, q = field[site], differ[site], image[site], image_two[site]
        residual[site] = u + kappa * w - sigma * q
        solved[site] = (1.0 - kappa) * b + sigma * u + dot(correction, vectors[site], NN)


def call(kernel, scalars, arrays, outs, name, cost=None, scratch=()):
    return pl.pallas_call(
        kernel,
        out_shape=[jax.ShapeDtypeStruct(shape, kind) for shape, kind in outs],
        in_specs=[pl.BlockSpec(memory_space=pltpu.SMEM)] * len(scalars)
        + [pl.BlockSpec(memory_space=pltpu.VMEM)] * len(arrays),
        out_specs=[pl.BlockSpec(memory_space=pltpu.VMEM)] * len(outs),
        compiler_params=pltpu.CompilerParams(vmem_limit_bytes=16 * 1024 * 1024),
        cost_estimate=cost,
        scratch_shapes=scratch,
        name=name,
    )(*scalars, *arrays)


def halo(field):
    sides = []
    for axis, step in SIDES:
        sides.append(lax.ppermute(field, axis, [((i + step) % 8, i) for i in range(8)]))
    return sides


def body(right_side, stencil, restrict, aggregate, coarsest_inverse):
    field = right_side[0, 0, 0]
    vectors = restrict[0, 0, 0]
    local = (field.shape, F32)
    label = aggregate.reshape(2)
    (weights,) = call(
        prepare_kernel,
        (),
        (stencil[0, 0, 0],),
        (((2, 4, 256, 256), BF16),),
        "prepare",
        pl.CostEstimate(flops=1 << 20, bytes_accessed=1 << 23, transcendentals=0),
    )
    image, differ = call(
        first_kernel,
        (),
        (field, *halo(field), weights),
        (local, local),
        "first_image",
    )
    early, inverse_high, inverse_low = call(
        early_kernel,
        (label,),
        (differ, image, vectors, coarsest_inverse),
        (((32, 128), F32), ((2048, 256), BF16), ((2048, 256), BF16)),
        "early_part",
        pl.CostEstimate(flops=1 << 20, bytes_accessed=1 << 22, transcendentals=0),
    )
    image_two, send = call(
        second_kernel,
        (),
        (differ, *halo(differ), weights, image, vectors, early),
        (local, ((8, 8, 128), F32)),
        "second_image",
    )
    recv = lax.all_to_all(send, BLOCK, 0, 0, tiled=True)
    (send,) = call(gather_kernel, (), (recv,), (((64, 8, 128), F32),), "block_sum")
    recv = lax.all_to_all(send, LATTICE, 0, 0, tiled=True)
    (send,) = call(
        coarse_kernel,
        (),
        (recv, inverse_high, inverse_low),
        (((32, 8, 128), F32),),
        "coarse_solve",
        scratch=[pltpu.VMEM((64, 8, 128), F32)] * 2,
    )
    recv = lax.all_to_all(send, ("a", "b", "Y", "c"), 0, 0, tiled=True)
    solved, residual = call(
        last_kernel,
        (),
        (recv, field, differ, image, image_two, vectors),
        (local, local),
        "last_update",
    )
    return solved[None, None, None], residual[None, None, None]


def solution(mesh):
    blocks = Mesh(mesh.devices.reshape(4, 2, 4, 2, 4, 2), ("T", "a", "Z", "b", "Y", "c"))
    spec = P(TA, GZ, XY)
    return jax.shard_map(
        body,
        mesh=blocks,
        in_specs=(spec, spec, spec, spec, P(XY)),
        out_specs=(spec, spec),
        check_vma=False,
    )
```

```python
import jax
import jax.numpy as jnp
from jax import lax
from jax.experimental import pallas as pl
from jax.experimental.pallas import tpu as pltpu
from jax.sharding import Mesh
from jax.sharding import PartitionSpec as P


TA, GZ, XY = ("T", "a"), ("Z", "b"), ("Y", "c")
COLUMN = ("a", "b", "Y", "c")
PLANE = ("T", "Z")
SIDES = [(GZ, 1), (TA, 1), (XY, 1), (GZ, -1), (TA, -1), (XY, -1)]
OFFSETS = [3, 1, 5, 4, 2, 6]
HIGHEST = lax.Precision.HIGHEST
F32 = jnp.float32
BF16 = jnp.bfloat16
NT = (((1,), (1,)), ((), ()))
NN = (((1,), (0,)), ((), ()))


def dot(left, right, dims):
    return lax.dot_general(left, right, dims, precision=HIGHEST, preferred_element_type=F32)


def split(value):
    high = value.astype(BF16)
    return high, (value - high.astype(F32)).astype(BF16)


def prepare_kernel(stencil, weights):
    rows = lax.broadcasted_iota(jnp.int32, (128, 128), 0)
    cols = lax.broadcasted_iota(jnp.int32, (128, 128), 1)
    unit = jnp.where(rows == cols, 1.0, 0.0).astype(F32)
    for site in range(2):
        for slot in range(8):
            if slot == 0:
                block = stencil[site, 0] - unit
            elif slot == 1:
                block = stencil[site, 7] + stencil[site, 8]
            else:
                block = stencil[site, OFFSETS[slot - 2]]
            high, low = split(jnp.transpose(block))
            start = 128 * (slot % 2)
            weights[site, slot // 2, start : start + 128, 0:128] = high
            weights[site, slot // 2, start : start + 128, 128:256] = low


def change(field, sides, weights, site):
    sides = [field[site], field[1 - site]] + [side[site] for side in sides]
    total = jnp.zeros((64, 256), F32)
    for pair in range(4):
        high, low = split(jnp.concatenate(sides[2 * pair : 2 * pair + 2], axis=1))
        both = jnp.concatenate([high, low], axis=0)
        total = total + lax.dot_general(
            both, weights[site, pair], NN, preferred_element_type=F32
        )
    half = total[0:32] + total[32:64]
    return half[:, 0:128] + half[:, 128:256]


def first_kernel(field, s0, s1, s2, s3, s4, s5, weights, image, differ):
    for site in range(2):
        value = change(field, (s0, s1, s2, s3, s4, s5), weights, site)
        image[site] = field[site] + value
        differ[site] = -value


def padded(vectors, start):
    rows = jnp.concatenate([vectors[0], vectors[1]], axis=1)
    parts = [rows]
    if start:
        parts.insert(0, jnp.zeros((start, 256), F32))
    if start < 96:
        parts.append(jnp.zeros((96 - start, 256), F32))
    return jnp.concatenate(parts, axis=0)


def inner(one, other):
    return jnp.sum(one[0] * other[0] + one[1] * other[1], axis=1, keepdims=True)


def wide(field):
    return jnp.concatenate([field[0], field[1]], axis=1)


def early_kernel(label, differ, image, vectors, packed):
    lane = lax.broadcasted_iota(jnp.int32, (32, 128), 1)
    value = dot(wide(differ), padded(vectors, 0), NT)
    value = value + dot(wide(image), padded(vectors, 32), NT)
    value = jnp.where(lane == 96, inner(image, image), value)
    value = jnp.where(lane == 97, inner(image, differ), value)
    packed[...] = jnp.where(lane == 101, label[0].astype(F32), value)


def second_kernel(
    differ, s0, s1, s2, s3, s4, s5, weights, image, vectors, early, image_two, send
):
    lane = lax.broadcasted_iota(jnp.int32, (32, 128), 1)
    values = []
    for site in range(2):
        value = differ[site] + change(differ, (s0, s1, s2, s3, s4, s5), weights, site)
        image_two[site] = value
        values.append(value)
    packed = early[...] + dot(wide(values), padded(vectors, 64), NT)
    packed = jnp.where(lane == 98, inner(image, values), packed)
    packed = jnp.where(lane == 99, inner(differ, values), packed)
    packed = jnp.where(lane == 100, inner(values, values), packed)
    for group in range(4):
        for other in range(8):
            send[8 * group + other] = packed[8 * group : 8 * group + 8]


def gather_kernel(recv, send):
    for y in range(4):
        total = recv[2 * y] + recv[2 * y + 1]
        for side in range(1, 4):
            total = total + (recv[8 * side + 2 * y] + recv[8 * side + 2 * y + 1])
        for other in range(16):
            send[other, y] = total


def coarse_kernel(recv, inverse, send, tiles, codes):
    lane = lax.broadcasted_iota(jnp.int32, (8, 128), 1)

    def pick(row, place):
        return jnp.sum(jnp.where(lane == place, row, 0.0), axis=1, keepdims=True)

    total = recv[0]
    for source in range(1, 64):
        total = total + recv[source]
    ww, wu, wq, qu, qq = [pick(total, 96 + place) for place in range(5)]
    first = wu / ww
    gamma = wq / ww
    sigma = (qu - gamma * wu) / (qq - gamma * wq)
    kappa = sigma * gamma - first
    group = (lane // 32).astype(F32)
    for source in range(64):
        part = recv[source]
        codes[source] = pick(part, 101) * 0.125 - group
        mixed = part + kappa * pltpu.roll(part, 96, 1) - sigma * pltpu.roll(part, 64, 1)
        mixed = jnp.where(lane < 32, mixed, 0.0)
        mixed = mixed + pltpu.roll(mixed, 32, 1)
        tiles[source] = mixed + pltpu.roll(mixed, 64, 1)
    rows = []
    for start in range(0, 16, 8):
        sums = [jnp.zeros((8, 128), F32) for _ in range(8)]
        for source in range(64):
            tile, code = tiles[source], codes[source]
            for place in range(8):
                sums[place] = sums[place] + jnp.where(code == 4.0 * (start + place), tile, 0.0)
        rows.extend(sums)
    high, low = split(jnp.concatenate(rows, axis=1))
    both = jnp.concatenate([high, low], axis=0)
    base = (8 * lax.axis_index(XY)).astype(F32)
    own = 16 * lax.axis_index("T") + 4 * lax.axis_index("Z")
    labels = [pick(recv[own + y], 101) * 0.125 - base for y in range(4)]
    scalars = jnp.where(lane == 32, sigma, jnp.where(lane == 33, kappa, 0.0))
    out = [jnp.zeros((8, 128), F32) for _ in range(4)]
    for part in range(2):
        held_high, held_low = split(inverse[128 * part : 128 * part + 128])
        value = lax.dot_general(both, held_high, NT, preferred_element_type=F32)
        value = value[0:8] + value[8:16]
        value = value + lax.dot_general(high, held_low, NT, preferred_element_type=F32)
        for place in range(4):
            row = pltpu.roll(value, 128 - 32 * place, 1) if place else value
            row = jnp.where(lane < 32, row, scalars)
            for y in range(4):
                out[y] = jnp.where(labels[y] == float(4 * part + place), row, out[y])
    for side in range(4):
        for y in range(4):
            for c in range(2):
                send[8 * side + 2 * y + c] = out[y]


def last_kernel(recv, field, differ, image, image_two, vectors, solved, residual):
    groups = []
    for group in range(4):
        total = recv[8 * group]
        for other in range(1, 8):
            total = total + recv[8 * group + other]
        groups.append(total)
    got = jnp.concatenate(groups, axis=0)
    correction = got[:, 0:32]
    sigma, kappa = got[:, 32:33], got[:, 33:34]
    for site in range(2):
        b, u, w, q = field[site], differ[site], image[site], image_two[site]
        residual[site] = u + kappa * w - sigma * q
        solved[site] = (1.0 - kappa) * b + sigma * u + dot(correction, vectors[site], NN)


def call(kernel, scalars, arrays, outs, name, cost=None, scratch=()):
    return pl.pallas_call(
        kernel,
        out_shape=[jax.ShapeDtypeStruct(shape, kind) for shape, kind in outs],
        in_specs=[pl.BlockSpec(memory_space=pltpu.SMEM)] * len(scalars)
        + [pl.BlockSpec(memory_space=pltpu.VMEM)] * len(arrays),
        out_specs=[pl.BlockSpec(memory_space=pltpu.VMEM)] * len(outs),
        compiler_params=pltpu.CompilerParams(vmem_limit_bytes=16 * 1024 * 1024),
        cost_estimate=cost,
        scratch_shapes=scratch,
        name=name,
    )(*scalars, *arrays)


def halo(field):
    sides = []
    for axis, step in SIDES:
        sides.append(lax.ppermute(field, axis, [((i + step) % 8, i) for i in range(8)]))
    return sides


def body(right_side, stencil, restrict, aggregate, coarsest_inverse):
    field = right_side[0, 0, 0]
    vectors = restrict[0, 0, 0]
    local = (field.shape, F32)
    label = aggregate.reshape(2)
    (weights,) = call(
        prepare_kernel,
        (),
        (stencil[0, 0, 0],),
        (((2, 4, 256, 256), BF16),),
        "prepare",
        pl.CostEstimate(flops=1 << 20, bytes_accessed=1 << 23, transcendentals=0),
    )
    image, differ = call(
        first_kernel,
        (),
        (field, *halo(field), weights),
        (local, local),
        "first_image",
    )
    (early,) = call(
        early_kernel, (label,), (differ, image, vectors), (((32, 128), F32),), "early_part"
    )
    image_two, send = call(
        second_kernel,
        (),
        (differ, *halo(differ), weights, image, vectors, early),
        (local, ((32, 8, 128), F32)),
        "second_image",
    )
    recv = lax.all_to_all(send, COLUMN, 0, 0, tiled=True)
    (send,) = call(gather_kernel, (), (recv,), (((16, 4, 8, 128), F32),), "block_sum")
    recv = lax.all_to_all(send, PLANE, 0, 0, tiled=True).reshape(64, 8, 128)
    (send,) = call(
        coarse_kernel,
        (),
        (recv, coarsest_inverse),
        (((32, 8, 128), F32),),
        "coarse_solve",
        scratch=[pltpu.VMEM((64, 8, 128), F32)] * 2,
    )
    recv = lax.all_to_all(send, COLUMN, 0, 0, tiled=True)
    solved, residual = call(
        last_kernel,
        (),
        (recv, field, differ, image, image_two, vectors),
        (local, local),
        "last_update",
    )
    return solved[None, None, None], residual[None, None, None]


def solution(mesh):
    blocks = Mesh(mesh.devices.reshape(4, 2, 4, 2, 4, 2), ("T", "a", "Z", "b", "Y", "c"))
    spec = P(TA, GZ, XY)
    return jax.shard_map(
        body,
        mesh=blocks,
        in_specs=(spec, spec, spec, spec, P(XY)),
        out_specs=(spec, spec),
        check_vma=False,
    )
```

```python
import jax
import jax.numpy as jnp
from jax import lax
from jax.experimental import pallas as pl
from jax.experimental.pallas import tpu as pltpu
from jax.sharding import Mesh
from jax.sharding import PartitionSpec as P


TA, GZ, XY = ("T", "a"), ("Z", "b"), ("Y", "c")
COLUMN = ("a", "b", "Y", "c")
PLANE = ("T", "Z")
INNER = [(0, 1), (1, 0), (2, 3), (3, 2), (4, 5), (5, 4), (6, 7), (7, 6)]
OUTER = [(1, 2), (2, 1), (3, 4), (4, 3), (5, 6), (6, 5), (7, 0), (0, 7)]
HIGHEST = lax.Precision.HIGHEST
F32 = jnp.float32
BF16 = jnp.bfloat16
NT = (((1,), (1,)), ((), ()))
NN = (((1,), (0,)), ((), ()))


def dot(left, right, dims):
    return lax.dot_general(left, right, dims, precision=HIGHEST, preferred_element_type=F32)


def split(value):
    high = value.astype(BF16)
    return high, (value - high.astype(F32)).astype(BF16)


def prepare_kernel(stencil, weights):
    a, b, c = (lax.axis_index(name) for name in ("a", "b", "c"))
    order = (4 - b, 2 - a, 6 - c, 3 + b, 1 + a, 5 + c)
    rows = lax.broadcasted_iota(jnp.int32, (128, 128), 0)
    cols = lax.broadcasted_iota(jnp.int32, (128, 128), 1)
    unit = jnp.where(rows == cols, 1.0, 0.0).astype(F32)
    for site in range(2):
        for slot in range(8):
            if slot == 0:
                block = stencil[site, 0] - unit
            elif slot == 1:
                block = stencil[site, 7] + stencil[site, 8]
            else:
                block = stencil[site, order[slot - 2]]
            high, low = split(jnp.transpose(block))
            start = 128 * (slot % 2)
            weights[site, slot // 2, start : start + 128, 0:128] = high
            weights[site, slot // 2, start : start + 128, 128:256] = low


def change(field, sides, weights, site):
    sides = [field[site], field[1 - site]] + [side[site] for side in sides]
    total = jnp.zeros((64, 256), F32)
    for pair in range(4):
        high, low = split(jnp.concatenate(sides[2 * pair : 2 * pair + 2], axis=1))
        both = jnp.concatenate([high, low], axis=0)
        total = total + lax.dot_general(
            both, weights[site, pair], NN, preferred_element_type=F32
        )
    half = total[0:32] + total[32:64]
    return half[:, 0:128] + half[:, 128:256]


def first_kernel(field, s0, s1, s2, s3, s4, s5, weights, image, differ):
    for site in range(2):
        value = change(field, (s0, s1, s2, s3, s4, s5), weights, site)
        image[site] = field[site] + value
        differ[site] = -value


def padded(vectors, start):
    rows = jnp.concatenate([vectors[0], vectors[1]], axis=1)
    parts = [rows]
    if start:
        parts.insert(0, jnp.zeros((start, 256), F32))
    if start < 96:
        parts.append(jnp.zeros((96 - start, 256), F32))
    return jnp.concatenate(parts, axis=0)


def inner(one, other):
    return jnp.sum(one[0] * other[0] + one[1] * other[1], axis=1, keepdims=True)


def wide(field):
    return jnp.concatenate([field[0], field[1]], axis=1)


def early_kernel(label, differ, image, vectors, packed):
    lane = lax.broadcasted_iota(jnp.int32, (32, 128), 1)
    value = dot(wide(differ), padded(vectors, 0), NT)
    value = value + dot(wide(image), padded(vectors, 32), NT)
    value = jnp.where(lane == 96, inner(image, image), value)
    value = jnp.where(lane == 97, inner(image, differ), value)
    packed[...] = jnp.where(lane == 101, label[0].astype(F32), value)


def second_kernel(
    differ, s0, s1, s2, s3, s4, s5, weights, image, vectors, early, image_two, send
):
    lane = lax.broadcasted_iota(jnp.int32, (32, 128), 1)
    values = []
    for site in range(2):
        value = differ[site] + change(differ, (s0, s1, s2, s3, s4, s5), weights, site)
        image_two[site] = value
        values.append(value)
    packed = early[...] + dot(wide(values), padded(vectors, 64), NT)
    packed = jnp.where(lane == 98, inner(image, values), packed)
    packed = jnp.where(lane == 99, inner(differ, values), packed)
    packed = jnp.where(lane == 100, inner(values, values), packed)
    for group in range(4):
        for other in range(8):
            send[8 * group + other] = packed[8 * group : 8 * group + 8]


def gather_kernel(recv, send):
    for y in range(4):
        total = recv[2 * y] + recv[2 * y + 1]
        for side in range(1, 4):
            total = total + (recv[8 * side + 2 * y] + recv[8 * side + 2 * y + 1])
        for other in range(16):
            send[other, y] = total


def coarse_kernel(recv, inverse, send, tiles, codes):
    lane = lax.broadcasted_iota(jnp.int32, (8, 128), 1)

    def pick(row, place):
        return jnp.sum(jnp.where(lane == place, row, 0.0), axis=1, keepdims=True)

    total = recv[0]
    for source in range(1, 64):
        total = total + recv[source]
    ww, wu, wq, qu, qq = [pick(total, 96 + place) for place in range(5)]
    first = wu / ww
    gamma = wq / ww
    sigma = (qu - gamma * wu) / (qq - gamma * wq)
    kappa = sigma * gamma - first
    group = (lane // 32).astype(F32)
    for source in range(64):
        part = recv[source]
        codes[source] = pick(part, 101) * 0.125 - group
        mixed = part + kappa * pltpu.roll(part, 96, 1) - sigma * pltpu.roll(part, 64, 1)
        mixed = jnp.where(lane < 32, mixed, 0.0)
        mixed = mixed + pltpu.roll(mixed, 32, 1)
        tiles[source] = mixed + pltpu.roll(mixed, 64, 1)
    rows = []
    for start in range(0, 16, 8):
        sums = [jnp.zeros((8, 128), F32) for _ in range(8)]
        for source in range(64):
            tile, code = tiles[source], codes[source]
            for place in range(8):
                sums[place] = sums[place] + jnp.where(code == 4.0 * (start + place), tile, 0.0)
        rows.extend(sums)
    high, low = split(jnp.concatenate(rows, axis=1))
    both = jnp.concatenate([high, low], axis=0)
    base = (8 * lax.axis_index(XY)).astype(F32)
    own = 16 * lax.axis_index("T") + 4 * lax.axis_index("Z")
    labels = [pick(recv[own + y], 101) * 0.125 - base for y in range(4)]
    scalars = jnp.where(lane == 32, sigma, jnp.where(lane == 33, kappa, 0.0))
    out = [jnp.zeros((8, 128), F32) for _ in range(4)]
    for part in range(2):
        held_high, held_low = split(inverse[128 * part : 128 * part + 128])
        value = lax.dot_general(both, held_high, NT, preferred_element_type=F32)
        value = value[0:8] + value[8:16]
        value = value + lax.dot_general(high, held_low, NT, preferred_element_type=F32)
        for place in range(4):
            row = pltpu.roll(value, 128 - 32 * place, 1) if place else value
            row = jnp.where(lane < 32, row, scalars)
            for y in range(4):
                out[y] = jnp.where(labels[y] == float(4 * part + place), row, out[y])
    for side in range(4):
        for y in range(4):
            for c in range(2):
                send[8 * side + 2 * y + c] = out[y]


def last_kernel(recv, field, differ, image, image_two, vectors, solved, residual):
    groups = []
    for group in range(4):
        total = recv[8 * group]
        for other in range(1, 8):
            total = total + recv[8 * group + other]
        groups.append(total)
    got = jnp.concatenate(groups, axis=0)
    correction = got[:, 0:32]
    sigma, kappa = got[:, 32:33], got[:, 33:34]
    for site in range(2):
        b, u, w, q = field[site], differ[site], image[site], image_two[site]
        residual[site] = u + kappa * w - sigma * q
        solved[site] = (1.0 - kappa) * b + sigma * u + dot(correction, vectors[site], NN)


def call(kernel, scalars, arrays, outs, name, cost=None, scratch=()):
    return pl.pallas_call(
        kernel,
        out_shape=[jax.ShapeDtypeStruct(shape, kind) for shape, kind in outs],
        in_specs=[pl.BlockSpec(memory_space=pltpu.SMEM)] * len(scalars)
        + [pl.BlockSpec(memory_space=pltpu.VMEM)] * len(arrays),
        out_specs=[pl.BlockSpec(memory_space=pltpu.VMEM)] * len(outs),
        compiler_params=pltpu.CompilerParams(vmem_limit_bytes=16 * 1024 * 1024),
        cost_estimate=cost,
        scratch_shapes=scratch,
        name=name,
    )(*scalars, *arrays)


def halo(field):
    sides = []
    for pairs in (OUTER, INNER):
        for axis in (GZ, TA, XY):
            sides.append(lax.ppermute(field, axis, pairs))
    return sides


def body(right_side, stencil, restrict, aggregate, coarsest_inverse):
    field = right_side[0, 0, 0]
    vectors = restrict[0, 0, 0]
    local = (field.shape, F32)
    label = aggregate.reshape(2)
    (weights,) = call(
        prepare_kernel,
        (),
        (stencil[0, 0, 0],),
        (((2, 4, 256, 256), BF16),),
        "prepare",
        pl.CostEstimate(flops=1 << 20, bytes_accessed=1 << 23, transcendentals=0),
    )
    image, differ = call(
        first_kernel,
        (),
        (field, *halo(field), weights),
        (local, local),
        "first_image",
    )
    (early,) = call(
        early_kernel, (label,), (differ, image, vectors), (((32, 128), F32),), "early_part"
    )
    image_two, send = call(
        second_kernel,
        (),
        (differ, *halo(differ), weights, image, vectors, early),
        (local, ((32, 8, 128), F32)),
        "second_image",
    )
    recv = lax.all_to_all(send, COLUMN, 0, 0, tiled=True)
    (send,) = call(gather_kernel, (), (recv,), (((16, 4, 8, 128), F32),), "block_sum")
    recv = lax.all_to_all(send, PLANE, 0, 0, tiled=True).reshape(64, 8, 128)
    (send,) = call(
        coarse_kernel,
        (),
        (recv, coarsest_inverse),
        (((32, 8, 128), F32),),
        "coarse_solve",
        scratch=[pltpu.VMEM((64, 8, 128), F32)] * 2,
    )
    recv = lax.all_to_all(send, COLUMN, 0, 0, tiled=True)
    solved, residual = call(
        last_kernel,
        (),
        (recv, field, differ, image, image_two, vectors),
        (local, local),
        "last_update",
    )
    return solved[None, None, None], residual[None, None, None]


def solution(mesh):
    blocks = Mesh(mesh.devices.reshape(4, 2, 4, 2, 4, 2), ("T", "a", "Z", "b", "Y", "c"))
    spec = P(TA, GZ, XY)
    return jax.shard_map(
        body,
        mesh=blocks,
        in_specs=(spec, spec, spec, spec, P(XY)),
        out_specs=(spec, spec),
        check_vma=False,
    )
```

```python
import jax
import jax.numpy as jnp
from jax import lax
from jax.experimental import pallas as pl
from jax.experimental.pallas import tpu as pltpu
from jax.sharding import Mesh
from jax.sharding import PartitionSpec as P


TA, GZ, XY = ("T", "a"), ("Z", "b"), ("Y", "c")
COLUMN = ("a", "b", "Y", "c")
PLANE = ("T", "Z")
SIDES = [(GZ, 1), (TA, 1), (XY, 1), (GZ, -1), (TA, -1), (XY, -1)]
OFFSETS = [3, 1, 5, 4, 2, 6]
HIGHEST = lax.Precision.HIGHEST
F32 = jnp.float32
BF16 = jnp.bfloat16
NT = (((1,), (1,)), ((), ()))
NN = (((1,), (0,)), ((), ()))


def dot(left, right, dims):
    return lax.dot_general(left, right, dims, precision=HIGHEST, preferred_element_type=F32)


def split(value):
    high = value.astype(BF16)
    return high, (value - high.astype(F32)).astype(BF16)


def prepare_kernel(stencil, weights):
    rows = lax.broadcasted_iota(jnp.int32, (128, 128), 0)
    cols = lax.broadcasted_iota(jnp.int32, (128, 128), 1)
    unit = jnp.where(rows == cols, 1.0, 0.0).astype(F32)
    for site in range(2):
        for slot in range(8):
            if slot == 0:
                block = stencil[site, 0] - unit
            elif slot == 1:
                block = stencil[site, 7] + stencil[site, 8]
            else:
                block = stencil[site, OFFSETS[slot - 2]]
            high, low = split(jnp.transpose(block))
            start = 128 * (slot % 2)
            weights[site, slot // 2, start : start + 128, 0:128] = high
            weights[site, slot // 2, start : start + 128, 128:256] = low


def change(field, sides, weights, site):
    sides = [field[site], field[1 - site]] + [side[site] for side in sides]
    total = jnp.zeros((64, 256), F32)
    for pair in range(4):
        high, low = split(jnp.concatenate(sides[2 * pair : 2 * pair + 2], axis=1))
        both = jnp.concatenate([high, low], axis=0)
        total = total + lax.dot_general(
            both, weights[site, pair], NN, preferred_element_type=F32
        )
    half = total[0:32] + total[32:64]
    return half[:, 0:128] + half[:, 128:256]


def first_kernel(field, s0, s1, s2, s3, s4, s5, weights, image, differ):
    for site in range(2):
        value = change(field, (s0, s1, s2, s3, s4, s5), weights, site)
        image[site] = field[site] + value
        differ[site] = -value


def padded(vectors, start):
    rows = jnp.concatenate([vectors[0], vectors[1]], axis=1)
    parts = [rows]
    if start:
        parts.insert(0, jnp.zeros((start, 256), F32))
    if start < 96:
        parts.append(jnp.zeros((96 - start, 256), F32))
    return jnp.concatenate(parts, axis=0)


def inner(one, other):
    return jnp.sum(one[0] * other[0] + one[1] * other[1], axis=1, keepdims=True)


def wide(field):
    return jnp.concatenate([field[0], field[1]], axis=1)


def early_kernel(label, differ, image, vectors, inverse, packed, inverse_high, inverse_low):
    lane = lax.broadcasted_iota(jnp.int32, (32, 128), 1)
    value = dot(wide(differ), padded(vectors, 0), NT)
    value = value + dot(wide(image), padded(vectors, 32), NT)
    value = jnp.where(lane == 96, inner(image, image), value)
    value = jnp.where(lane == 97, inner(image, differ), value)
    packed[...] = jnp.where(lane == 101, label[0].astype(F32), value)
    high, low = split(inverse[...])
    inverse_high[...] = high
    inverse_low[...] = low


def second_kernel(
    differ, s0, s1, s2, s3, s4, s5, weights, image, vectors, early, image_two, send
):
    lane = lax.broadcasted_iota(jnp.int32, (32, 128), 1)
    values = []
    for site in range(2):
        value = differ[site] + change(differ, (s0, s1, s2, s3, s4, s5), weights, site)
        image_two[site] = value
        values.append(value)
    packed = early[...] + dot(wide(values), padded(vectors, 64), NT)
    packed = jnp.where(lane == 98, inner(image, values), packed)
    packed = jnp.where(lane == 99, inner(differ, values), packed)
    packed = jnp.where(lane == 100, inner(values, values), packed)
    for group in range(4):
        for other in range(8):
            send[8 * group + other] = packed[8 * group : 8 * group + 8]


def gather_kernel(recv, send):
    for y in range(4):
        total = recv[2 * y] + recv[2 * y + 1]
        for side in range(1, 4):
            total = total + (recv[8 * side + 2 * y] + recv[8 * side + 2 * y + 1])
        for other in range(16):
            send[other, y] = total


def turns(value):
    return [value] + [pltpu.roll(value, 32 * place, 1) for place in range(1, 4)]


def pack(rolled, place, row, lane):
    turned = jnp.zeros((8, 128), F32)
    for right in range(4):
        group = -right % 4
        here = jnp.logical_and(row % 4 == right, lane // 32 == group)
        turned = jnp.where(here, rolled[(group - place) % 4], turned)
    low = jnp.sum(jnp.where(row < 4, turned, 0.0), axis=0, keepdims=True)
    high = jnp.sum(jnp.where(row < 4, 0.0, turned), axis=0, keepdims=True)
    return low, high


def coarse_kernel(recv, inverse_high, inverse_low, send, rows):
    lane = lax.broadcasted_iota(jnp.int32, (8, 128), 1)
    row = lax.broadcasted_iota(jnp.int32, (8, 128), 0)

    def pick(value, place):
        return jnp.sum(jnp.where(lane == place, value, 0.0), axis=1, keepdims=True)

    numbers = []
    for start in range(0, 64, 8):
        tops = jnp.concatenate([recv[start + place, 0:1, :] for place in range(8)], axis=0)
        numbers.append((pick(tops, 101) * 0.125).astype(jnp.int32))
    total = recv[0]
    for source in range(1, 64):
        total = total + recv[source]
    ww, wu, wq, qu, qq = [pick(total, 96 + place) for place in range(5)]
    first = wu / ww
    gamma = wq / ww
    sigma = (qu - gamma * wu) / (qq - gamma * wq)
    kappa = sigma * gamma - first
    group = lane // 32
    for source in range(64):
        number = numbers[source // 8][source % 8, 0]
        part = recv[source]
        mixed = part + kappa * pltpu.roll(part, 96, 1) - sigma * pltpu.roll(part, 64, 1)
        mixed = pltpu.roll(mixed, 32 * (number % 4), 1)
        pltpu.store(rows.at[number // 4], mixed, mask=group == number % 4)
    high, low = split(jnp.concatenate([rows[place] for place in range(16)], axis=1))
    both = jnp.concatenate([high, low], axis=0)
    base = 8 * lax.axis_index(XY)
    own = 16 * lax.axis_index("T") + 4 * lax.axis_index("Z")
    labels = [pick(recv[own + y], 101)[0:1] * 0.125 - base.astype(F32) for y in range(4)]
    turned = jnp.where(lane == row, sigma, jnp.where(lane == row + 8, kappa, 0.0))
    scalars = jnp.sum(turned, axis=0, keepdims=True)
    out = [[jnp.zeros((1, 128), F32) for _ in range(3)] for _ in range(4)]
    for half in range(2):
        begin = 128 * half
        value = lax.dot_general(
            both, inverse_high[begin : begin + 128], NT, preferred_element_type=F32
        )
        value = value[0:8] + value[8:16]
        value = value + lax.dot_general(
            high, inverse_low[begin : begin + 128], NT, preferred_element_type=F32
        )
        rolled = turns(value)
        for place in range(4):
            packed = (*pack(rolled, place, row, lane), scalars)
            for y in range(4):
                for line in range(3):
                    out[y][line] = jnp.where(
                        labels[y] == float(4 * half + place), packed[line], out[y][line]
                    )
    for y in range(4):
        block = jnp.concatenate([*out[y], jnp.zeros((1, 128), F32)], axis=0)
        for side in range(4):
            for c in range(2):
                send[8 * side + 2 * y + c] = block


def last_kernel(recv, field, differ, image, image_two, vectors, solved, residual):
    lane = lax.broadcasted_iota(jnp.int32, (8, 128), 1)
    row = lax.broadcasted_iota(jnp.int32, (8, 128), 0)
    parts, sigmas, kappas = [], [], []
    for group in range(4):
        total = recv[8 * group]
        for other in range(1, 8):
            total = total + recv[8 * group + other]
        lines = jnp.where(row < 4, total[0:1], total[1:2])
        rolled = turns(lines)
        for right in range(1, 4):
            lines = jnp.where(row % 4 == right, rolled[right], lines)
        parts.append(lines)
        scalars = jnp.broadcast_to(total[2:3], (8, 128))
        sigmas.append(jnp.sum(jnp.where(lane == row, scalars, 0.0), axis=1, keepdims=True))
        kappas.append(jnp.sum(jnp.where(lane == row + 8, scalars, 0.0), axis=1, keepdims=True))
    correction = jnp.concatenate(parts, axis=0)[:, 0:32]
    sigma, kappa = jnp.concatenate(sigmas, axis=0), jnp.concatenate(kappas, axis=0)
    for site in range(2):
        b, u, w, q = field[site], differ[site], image[site], image_two[site]
        residual[site] = u + kappa * w - sigma * q
        solved[site] = (1.0 - kappa) * b + sigma * u + dot(correction, vectors[site], NN)


def call(kernel, scalars, arrays, outs, name, cost=None, scratch=()):
    return pl.pallas_call(
        kernel,
        out_shape=[jax.ShapeDtypeStruct(shape, kind) for shape, kind in outs],
        in_specs=[pl.BlockSpec(memory_space=pltpu.SMEM)] * len(scalars)
        + [pl.BlockSpec(memory_space=pltpu.VMEM)] * len(arrays),
        out_specs=[pl.BlockSpec(memory_space=pltpu.VMEM)] * len(outs),
        compiler_params=pltpu.CompilerParams(vmem_limit_bytes=16 * 1024 * 1024),
        cost_estimate=cost,
        scratch_shapes=scratch,
        name=name,
    )(*scalars, *arrays)


def halo(field):
    sides = []
    for axis, step in SIDES:
        sides.append(lax.ppermute(field, axis, [((i + step) % 8, i) for i in range(8)]))
    return sides


def body(right_side, stencil, restrict, aggregate, coarsest_inverse):
    field = right_side[0, 0, 0]
    vectors = restrict[0, 0, 0]
    local = (field.shape, F32)
    label = aggregate.reshape(2)
    (weights,) = call(
        prepare_kernel,
        (),
        (stencil[0, 0, 0],),
        (((2, 4, 256, 256), BF16),),
        "prepare",
        pl.CostEstimate(flops=1 << 20, bytes_accessed=1 << 23, transcendentals=0),
    )
    image, differ = call(
        first_kernel,
        (),
        (field, *halo(field), weights),
        (local, local),
        "first_image",
    )
    early, inverse_high, inverse_low = call(
        early_kernel,
        (label,),
        (differ, image, vectors, coarsest_inverse),
        (((32, 128), F32), ((256, 2048), BF16), ((256, 2048), BF16)),
        "early_part",
        pl.CostEstimate(flops=1 << 20, bytes_accessed=1 << 22, transcendentals=0),
    )
    image_two, send = call(
        second_kernel,
        (),
        (differ, *halo(differ), weights, image, vectors, early),
        (local, ((32, 8, 128), F32)),
        "second_image",
    )
    recv = lax.all_to_all(send, COLUMN, 0, 0, tiled=True)
    (send,) = call(gather_kernel, (), (recv,), (((16, 4, 8, 128), F32),), "block_sum")
    recv = lax.all_to_all(send, PLANE, 0, 0, tiled=True).reshape(64, 8, 128)
    (send,) = call(
        coarse_kernel,
        (),
        (recv, inverse_high, inverse_low),
        (((32, 4, 128), F32),),
        "coarse_solve",
        scratch=[pltpu.VMEM((16, 8, 128), F32)],
    )
    recv = lax.all_to_all(send, COLUMN, 0, 0, tiled=True)
    solved, residual = call(
        last_kernel,
        (),
        (recv, field, differ, image, image_two, vectors),
        (local, local),
        "last_update",
    )
    return solved[None, None, None], residual[None, None, None]


def solution(mesh):
    blocks = Mesh(mesh.devices.reshape(4, 2, 4, 2, 4, 2), ("T", "a", "Z", "b", "Y", "c"))
    spec = P(TA, GZ, XY)
    return jax.shard_map(
        body,
        mesh=blocks,
        in_specs=(spec, spec, spec, spec, P(XY)),
        out_specs=(spec, spec),
        check_vma=False,
    )
```

```python
import jax
import jax.numpy as jnp
from jax import lax
from jax.experimental import pallas as pl
from jax.experimental.pallas import tpu as pltpu
from jax.sharding import Mesh
from jax.sharding import PartitionSpec as P


TA, GZ, XY = ("T", "a"), ("Z", "b"), ("Y", "c")
COLUMN = ("a", "b", "Y", "c")
BLOCK = ("a", "b", "c")
LATTICE = ("T", "Z", "Y")
SIDES = [(GZ, 1), (TA, 1), (XY, 1), (GZ, -1), (TA, -1), (XY, -1)]
OFFSETS = [3, 1, 5, 4, 2, 6]
HIGHEST = lax.Precision.HIGHEST
F32 = jnp.float32
BF16 = jnp.bfloat16
NT = (((1,), (1,)), ((), ()))
NN = (((1,), (0,)), ((), ()))


def dot(left, right, dims):
    return lax.dot_general(left, right, dims, precision=HIGHEST, preferred_element_type=F32)


def split(value):
    high = value.astype(BF16)
    return high, (value - high.astype(F32)).astype(BF16)


def prepare_kernel(stencil, weights):
    rows = lax.broadcasted_iota(jnp.int32, (128, 128), 0)
    cols = lax.broadcasted_iota(jnp.int32, (128, 128), 1)
    unit = jnp.where(rows == cols, 1.0, 0.0).astype(F32)
    for site in range(2):
        for slot in range(8):
            if slot == 0:
                block = stencil[site, 0] - unit
            elif slot == 1:
                block = stencil[site, 7] + stencil[site, 8]
            else:
                block = stencil[site, OFFSETS[slot - 2]]
            high, low = split(jnp.transpose(block))
            start = 128 * (slot % 2)
            weights[site, slot // 2, start : start + 128, 0:128] = high
            weights[site, slot // 2, start : start + 128, 128:256] = low


def change(field, sides, weights, site):
    sides = [field[site], field[1 - site]] + [side[site] for side in sides]
    total = jnp.zeros((64, 256), F32)
    for pair in range(4):
        high, low = split(jnp.concatenate(sides[2 * pair : 2 * pair + 2], axis=1))
        both = jnp.concatenate([high, low], axis=0)
        total = total + lax.dot_general(
            both, weights[site, pair], NN, preferred_element_type=F32
        )
    half = total[0:32] + total[32:64]
    return half[:, 0:128] + half[:, 128:256]


def first_kernel(field, s0, s1, s2, s3, s4, s5, weights, image, differ):
    for site in range(2):
        value = change(field, (s0, s1, s2, s3, s4, s5), weights, site)
        image[site] = field[site] + value
        differ[site] = -value


def padded(vectors, start):
    rows = jnp.concatenate([vectors[0], vectors[1]], axis=1)
    parts = [rows]
    if start:
        parts.insert(0, jnp.zeros((start, 256), F32))
    if start < 96:
        parts.append(jnp.zeros((96 - start, 256), F32))
    return jnp.concatenate(parts, axis=0)


def inner(one, other):
    return jnp.sum(one[0] * other[0] + one[1] * other[1], axis=1, keepdims=True)


def wide(field):
    return jnp.concatenate([field[0], field[1]], axis=1)


def early_kernel(label, differ, image, vectors, inverse, packed, inverse_high, inverse_low):
    lane = lax.broadcasted_iota(jnp.int32, (32, 128), 1)
    value = dot(wide(differ), padded(vectors, 0), NT)
    value = value + dot(wide(image), padded(vectors, 32), NT)
    value = jnp.where(lane == 96, inner(image, image), value)
    value = jnp.where(lane == 97, inner(image, differ), value)
    packed[...] = jnp.where(lane == 101, label[0].astype(F32), value)
    high, low = split(inverse[...])
    inverse_high[...] = high
    inverse_low[...] = low


def second_kernel(
    differ, s0, s1, s2, s3, s4, s5, weights, image, vectors, early, image_two, send
):
    lane = lax.broadcasted_iota(jnp.int32, (32, 128), 1)
    values = []
    for site in range(2):
        value = differ[site] + change(differ, (s0, s1, s2, s3, s4, s5), weights, site)
        image_two[site] = value
        values.append(value)
    packed = early[...] + dot(wide(values), padded(vectors, 64), NT)
    packed = jnp.where(lane == 98, inner(image, values), packed)
    packed = jnp.where(lane == 99, inner(differ, values), packed)
    packed = jnp.where(lane == 100, inner(values, values), packed)
    for group in range(4):
        for c in range(2):
            send[2 * group + c] = packed[8 * group : 8 * group + 8]


def gather_kernel(recv, send):
    total = recv[0]
    for other in range(1, 8):
        total = total + recv[other]
    for other in range(64):
        send[other] = total


def turns(value):
    return [value] + [pltpu.roll(value, 32 * place, 1) for place in range(1, 4)]


def pack(rolled, place, row, lane):
    turned = jnp.zeros((8, 128), F32)
    for right in range(4):
        group = -right % 4
        here = jnp.logical_and(row % 4 == right, lane // 32 == group)
        turned = jnp.where(here, rolled[(group - place) % 4], turned)
    low = jnp.sum(jnp.where(row < 4, turned, 0.0), axis=0, keepdims=True)
    high = jnp.sum(jnp.where(row < 4, 0.0, turned), axis=0, keepdims=True)
    return low, high


def coarse_kernel(recv, inverse_high, inverse_low, send, rows):
    lane = lax.broadcasted_iota(jnp.int32, (8, 128), 1)
    row = lax.broadcasted_iota(jnp.int32, (8, 128), 0)

    def pick(value, place):
        return jnp.sum(jnp.where(lane == place, value, 0.0), axis=1, keepdims=True)

    numbers = []
    for start in range(0, 64, 8):
        tops = jnp.concatenate([recv[start + place, 0:1, :] for place in range(8)], axis=0)
        numbers.append((pick(tops, 101) * 0.125).astype(jnp.int32))
    total = recv[0]
    for source in range(1, 64):
        total = total + recv[source]
    ww, wu, wq, qu, qq = [pick(total, 96 + place) for place in range(5)]
    first = wu / ww
    gamma = wq / ww
    sigma = (qu - gamma * wu) / (qq - gamma * wq)
    kappa = sigma * gamma - first
    group = lane // 32
    for source in range(64):
        number = numbers[source // 8][source % 8, 0]
        part = recv[source]
        mixed = part + kappa * pltpu.roll(part, 96, 1) - sigma * pltpu.roll(part, 64, 1)
        mixed = pltpu.roll(mixed, 32 * (number % 4), 1)
        pltpu.store(rows.at[number // 4], mixed, mask=group == number % 4)
    high, low = split(jnp.concatenate([rows[place] for place in range(16)], axis=1))
    both = jnp.concatenate([high, low], axis=0)
    base = 8 * lax.axis_index(XY)
    own = 16 * lax.axis_index("T") + 4 * lax.axis_index("Z")
    labels = [pick(recv[own + y], 101)[0:1] * 0.125 - base.astype(F32) for y in range(4)]
    turned = jnp.where(lane == row, sigma, jnp.where(lane == row + 8, kappa, 0.0))
    scalars = jnp.sum(turned, axis=0, keepdims=True)
    out = [[jnp.zeros((1, 128), F32) for _ in range(3)] for _ in range(4)]
    for half in range(2):
        begin = 128 * half
        value = lax.dot_general(
            both, inverse_high[begin : begin + 128], NT, preferred_element_type=F32
        )
        value = value[0:8] + value[8:16]
        value = value + lax.dot_general(
            high, inverse_low[begin : begin + 128], NT, preferred_element_type=F32
        )
        rolled = turns(value)
        for place in range(4):
            packed = (*pack(rolled, place, row, lane), scalars)
            for y in range(4):
                for line in range(3):
                    out[y][line] = jnp.where(
                        labels[y] == float(4 * half + place), packed[line], out[y][line]
                    )
    for y in range(4):
        block = jnp.concatenate([*out[y], jnp.zeros((1, 128), F32)], axis=0)
        for side in range(4):
            for c in range(2):
                send[8 * side + 2 * y + c] = block


def last_kernel(recv, field, differ, image, image_two, vectors, solved, residual):
    lane = lax.broadcasted_iota(jnp.int32, (8, 128), 1)
    row = lax.broadcasted_iota(jnp.int32, (8, 128), 0)
    parts, sigmas, kappas = [], [], []
    for group in range(4):
        total = recv[8 * group]
        for other in range(1, 8):
            total = total + recv[8 * group + other]
        lines = jnp.where(row < 4, total[0:1], total[1:2])
        rolled = turns(lines)
        for right in range(1, 4):
            lines = jnp.where(row % 4 == right, rolled[right], lines)
        parts.append(lines)
        scalars = jnp.broadcast_to(total[2:3], (8, 128))
        sigmas.append(jnp.sum(jnp.where(lane == row, scalars, 0.0), axis=1, keepdims=True))
        kappas.append(jnp.sum(jnp.where(lane == row + 8, scalars, 0.0), axis=1, keepdims=True))
    correction = jnp.concatenate(parts, axis=0)[:, 0:32]
    sigma, kappa = jnp.concatenate(sigmas, axis=0), jnp.concatenate(kappas, axis=0)
    for site in range(2):
        b, u, w, q = field[site], differ[site], image[site], image_two[site]
        residual[site] = u + kappa * w - sigma * q
        solved[site] = (1.0 - kappa) * b + sigma * u + dot(correction, vectors[site], NN)


def call(kernel, scalars, arrays, outs, name, cost=None, scratch=()):
    return pl.pallas_call(
        kernel,
        out_shape=[jax.ShapeDtypeStruct(shape, kind) for shape, kind in outs],
        in_specs=[pl.BlockSpec(memory_space=pltpu.SMEM)] * len(scalars)
        + [pl.BlockSpec(memory_space=pltpu.VMEM)] * len(arrays),
        out_specs=[pl.BlockSpec(memory_space=pltpu.VMEM)] * len(outs),
        compiler_params=pltpu.CompilerParams(vmem_limit_bytes=16 * 1024 * 1024),
        cost_estimate=cost,
        scratch_shapes=scratch,
        name=name,
    )(*scalars, *arrays)


def halo(field):
    sides = []
    for axis, step in SIDES:
        sides.append(lax.ppermute(field, axis, [((i + step) % 8, i) for i in range(8)]))
    return sides


def body(right_side, stencil, restrict, aggregate, coarsest_inverse):
    field = right_side[0, 0, 0]
    vectors = restrict[0, 0, 0]
    local = (field.shape, F32)
    label = aggregate.reshape(2)
    (weights,) = call(
        prepare_kernel,
        (),
        (stencil[0, 0, 0],),
        (((2, 4, 256, 256), BF16),),
        "prepare",
        pl.CostEstimate(flops=1 << 20, bytes_accessed=1 << 23, transcendentals=0),
    )
    image, differ = call(
        first_kernel,
        (),
        (field, *halo(field), weights),
        (local, local),
        "first_image",
    )
    early, inverse_high, inverse_low = call(
        early_kernel,
        (label,),
        (differ, image, vectors, coarsest_inverse),
        (((32, 128), F32), ((256, 2048), BF16), ((256, 2048), BF16)),
        "early_part",
        pl.CostEstimate(flops=1 << 20, bytes_accessed=1 << 22, transcendentals=0),
    )
    image_two, send = call(
        second_kernel,
        (),
        (differ, *halo(differ), weights, image, vectors, early),
        (local, ((8, 8, 128), F32)),
        "second_image",
    )
    recv = lax.all_to_all(send, BLOCK, 0, 0, tiled=True)
    (send,) = call(gather_kernel, (), (recv,), (((64, 8, 128), F32),), "block_sum")
    recv = lax.all_to_all(send, LATTICE, 0, 0, tiled=True)
    (send,) = call(
        coarse_kernel,
        (),
        (recv, inverse_high, inverse_low),
        (((32, 4, 128), F32),),
        "coarse_solve",
        scratch=[pltpu.VMEM((16, 8, 128), F32)],
    )
    recv = lax.all_to_all(send, COLUMN, 0, 0, tiled=True)
    solved, residual = call(
        last_kernel,
        (),
        (recv, field, differ, image, image_two, vectors),
        (local, local),
        "last_update",
    )
    return solved[None, None, None], residual[None, None, None]


def solution(mesh):
    blocks = Mesh(mesh.devices.reshape(4, 2, 4, 2, 4, 2), ("T", "a", "Z", "b", "Y", "c"))
    spec = P(TA, GZ, XY)
    return jax.shard_map(
        body,
        mesh=blocks,
        in_specs=(spec, spec, spec, spec, P(XY)),
        out_specs=(spec, spec),
        check_vma=False,
    )
```

```python
import jax
import jax.numpy as jnp
from jax import lax
from jax.experimental import pallas as pl
from jax.experimental.pallas import tpu as pltpu
from jax.sharding import Mesh
from jax.sharding import PartitionSpec as P


TA, GZ, XY = ("T", "a"), ("Z", "b"), ("Y", "c")
COLUMN = ("a", "b", "Y", "c")
BLOCK = ("a", "b", "c")
LATTICE = ("T", "Z", "Y")
SIDES = [(TA, 1), (TA, -1), (GZ, 1), (GZ, -1), (XY, 1), (XY, -1)]
OFFSETS = [1, 2, 3, 4, 5, 6]
HIGHEST = lax.Precision.HIGHEST
F32 = jnp.float32
BF16 = jnp.bfloat16
NT = (((1,), (1,)), ((), ()))
NN = (((1,), (0,)), ((), ()))


def dot(left, right, dims):
    return lax.dot_general(left, right, dims, precision=HIGHEST, preferred_element_type=F32)


def split(value):
    high = value.astype(BF16)
    return high, (value - high.astype(F32)).astype(BF16)


def prepare_kernel(stencil, weights):
    rows = lax.broadcasted_iota(jnp.int32, (128, 128), 0)
    cols = lax.broadcasted_iota(jnp.int32, (128, 128), 1)
    unit = jnp.where(rows == cols, 1.0, 0.0).astype(F32)
    for site in range(2):
        for slot in range(8):
            if slot == 0:
                block = stencil[site, 0] - unit
            elif slot == 1:
                block = stencil[site, 7] + stencil[site, 8]
            else:
                block = stencil[site, OFFSETS[slot - 2]]
            high, low = split(jnp.transpose(block))
            start = 128 * (slot % 2)
            weights[site, slot // 2, start : start + 128, 0:128] = high
            weights[site, slot // 2, start : start + 128, 128:256] = low


def change(field, sides, weights, site):
    sides = [field[site], field[1 - site]] + [side[site] for side in sides]
    total = jnp.zeros((64, 256), F32)
    for pair in range(4):
        high, low = split(jnp.concatenate(sides[2 * pair : 2 * pair + 2], axis=1))
        both = jnp.concatenate([high, low], axis=0)
        total = total + lax.dot_general(
            both, weights[site, pair], NN, preferred_element_type=F32
        )
    half = total[0:32] + total[32:64]
    return half[:, 0:128] + half[:, 128:256]


def first_kernel(field, s0, s1, s2, s3, s4, s5, weights, image, differ):
    for site in range(2):
        value = change(field, (s0, s1, s2, s3, s4, s5), weights, site)
        image[site] = field[site] + value
        differ[site] = -value


def padded(vectors, start):
    rows = jnp.concatenate([vectors[0], vectors[1]], axis=1)
    parts = [rows]
    if start:
        parts.insert(0, jnp.zeros((start, 256), F32))
    if start < 96:
        parts.append(jnp.zeros((96 - start, 256), F32))
    return jnp.concatenate(parts, axis=0)


def inner(one, other):
    return jnp.sum(one[0] * other[0] + one[1] * other[1], axis=1, keepdims=True)


def wide(field):
    return jnp.concatenate([field[0], field[1]], axis=1)


def early_kernel(label, differ, image, vectors, inverse, packed, inverse_high, inverse_low):
    lane = lax.broadcasted_iota(jnp.int32, (32, 128), 1)
    value = dot(wide(differ), padded(vectors, 0), NT)
    value = value + dot(wide(image), padded(vectors, 32), NT)
    value = jnp.where(lane == 96, inner(image, image), value)
    value = jnp.where(lane == 97, inner(image, differ), value)
    packed[...] = jnp.where(lane == 101, label[0].astype(F32), value)
    high, low = split(inverse[...])
    inverse_high[...] = high
    inverse_low[...] = low


def second_kernel(
    differ, s0, s1, s2, s3, s4, s5, weights, image, vectors, early, image_two, send
):
    lane = lax.broadcasted_iota(jnp.int32, (32, 128), 1)
    values = []
    for site in range(2):
        value = differ[site] + change(differ, (s0, s1, s2, s3, s4, s5), weights, site)
        image_two[site] = value
        values.append(value)
    packed = early[...] + dot(wide(values), padded(vectors, 64), NT)
    packed = jnp.where(lane == 98, inner(image, values), packed)
    packed = jnp.where(lane == 99, inner(differ, values), packed)
    packed = jnp.where(lane == 100, inner(values, values), packed)
    for group in range(4):
        for c in range(2):
            send[2 * group + c] = packed[8 * group : 8 * group + 8]


def gather_kernel(recv, send):
    total = recv[0]
    for other in range(1, 8):
        total = total + recv[other]
    for other in range(64):
        send[other] = total


def turns(value):
    return [value] + [pltpu.roll(value, 32 * place, 1) for place in range(1, 4)]


def pack(rolled, place, row, lane):
    turned = jnp.zeros((8, 128), F32)
    for right in range(4):
        group = -right % 4
        here = jnp.logical_and(row % 4 == right, lane // 32 == group)
        turned = jnp.where(here, rolled[(group - place) % 4], turned)
    low = jnp.sum(jnp.where(row < 4, turned, 0.0), axis=0, keepdims=True)
    high = jnp.sum(jnp.where(row < 4, 0.0, turned), axis=0, keepdims=True)
    return low, high


def coarse_kernel(recv, inverse_high, inverse_low, send, rows):
    lane = lax.broadcasted_iota(jnp.int32, (8, 128), 1)
    row = lax.broadcasted_iota(jnp.int32, (8, 128), 0)

    def pick(value, place):
        return jnp.sum(jnp.where(lane == place, value, 0.0), axis=1, keepdims=True)

    numbers = []
    for start in range(0, 64, 8):
        tops = jnp.concatenate([recv[start + place, 0:1, :] for place in range(8)], axis=0)
        numbers.append((pick(tops, 101) * 0.125).astype(jnp.int32))
    total = recv[0]
    for source in range(1, 64):
        total = total + recv[source]
    ww, wu, wq, qu, qq = [pick(total, 96 + place) for place in range(5)]
    first = wu / ww
    gamma = wq / ww
    sigma = (qu - gamma * wu) / (qq - gamma * wq)
    kappa = sigma * gamma - first
    group = lane // 32
    for source in range(64):
        number = numbers[source // 8][source % 8, 0]
        part = recv[source]
        mixed = part + kappa * pltpu.roll(part, 96, 1) - sigma * pltpu.roll(part, 64, 1)
        mixed = pltpu.roll(mixed, 32 * (number % 4), 1)
        pltpu.store(rows.at[number // 4], mixed, mask=group == number % 4)
    high, low = split(jnp.concatenate([rows[place] for place in range(16)], axis=1))
    both = jnp.concatenate([high, low], axis=0)
    base = 8 * lax.axis_index(XY)
    own = 16 * lax.axis_index("T") + 4 * lax.axis_index("Z")
    labels = [pick(recv[own + y], 101)[0:1] * 0.125 - base.astype(F32) for y in range(4)]
    turned = jnp.where(lane == row, sigma, jnp.where(lane == row + 8, kappa, 0.0))
    scalars = jnp.sum(turned, axis=0, keepdims=True)
    out = [[jnp.zeros((1, 128), F32) for _ in range(3)] for _ in range(4)]
    for half in range(2):
        begin = 128 * half
        value = lax.dot_general(
            both, inverse_high[begin : begin + 128], NT, preferred_element_type=F32
        )
        value = value[0:8] + value[8:16]
        value = value + lax.dot_general(
            high, inverse_low[begin : begin + 128], NT, preferred_element_type=F32
        )
        rolled = turns(value)
        for place in range(4):
            packed = (*pack(rolled, place, row, lane), scalars)
            for y in range(4):
                for line in range(3):
                    out[y][line] = jnp.where(
                        labels[y] == float(4 * half + place), packed[line], out[y][line]
                    )
    for y in range(4):
        block = jnp.concatenate([*out[y], jnp.zeros((1, 128), F32)], axis=0)
        for side in range(4):
            for c in range(2):
                send[8 * side + 2 * y + c] = block


def last_kernel(recv, field, differ, image, image_two, vectors, solved, residual):
    lane = lax.broadcasted_iota(jnp.int32, (8, 128), 1)
    row = lax.broadcasted_iota(jnp.int32, (8, 128), 0)
    parts, sigmas, kappas = [], [], []
    for group in range(4):
        total = recv[8 * group]
        for other in range(1, 8):
            total = total + recv[8 * group + other]
        lines = jnp.where(row < 4, total[0:1], total[1:2])
        rolled = turns(lines)
        for right in range(1, 4):
            lines = jnp.where(row % 4 == right, rolled[right], lines)
        parts.append(lines)
        scalars = jnp.broadcast_to(total[2:3], (8, 128))
        sigmas.append(jnp.sum(jnp.where(lane == row, scalars, 0.0), axis=1, keepdims=True))
        kappas.append(jnp.sum(jnp.where(lane == row + 8, scalars, 0.0), axis=1, keepdims=True))
    correction = jnp.concatenate(parts, axis=0)[:, 0:32]
    sigma, kappa = jnp.concatenate(sigmas, axis=0), jnp.concatenate(kappas, axis=0)
    for site in range(2):
        b, u, w, q = field[site], differ[site], image[site], image_two[site]
        residual[site] = u + kappa * w - sigma * q
        solved[site] = (1.0 - kappa) * b + sigma * u + dot(correction, vectors[site], NN)


def call(kernel, scalars, arrays, outs, name, cost=None, scratch=()):
    return pl.pallas_call(
        kernel,
        out_shape=[jax.ShapeDtypeStruct(shape, kind) for shape, kind in outs],
        in_specs=[pl.BlockSpec(memory_space=pltpu.SMEM)] * len(scalars)
        + [pl.BlockSpec(memory_space=pltpu.VMEM)] * len(arrays),
        out_specs=[pl.BlockSpec(memory_space=pltpu.VMEM)] * len(outs),
        compiler_params=pltpu.CompilerParams(vmem_limit_bytes=16 * 1024 * 1024),
        cost_estimate=cost,
        scratch_shapes=scratch,
        name=name,
    )(*scalars, *arrays)


def halo(field):
    sides = []
    for axis, step in SIDES:
        sides.append(lax.ppermute(field, axis, [((i + step) % 8, i) for i in range(8)]))
    return sides


def body(right_side, stencil, restrict, aggregate, coarsest_inverse):
    field = right_side[0, 0, 0]
    vectors = restrict[0, 0, 0]
    local = (field.shape, F32)
    label = aggregate.reshape(2)
    (weights,) = call(
        prepare_kernel,
        (),
        (stencil[0, 0, 0],),
        (((2, 4, 256, 256), BF16),),
        "prepare",
        pl.CostEstimate(flops=1 << 20, bytes_accessed=1 << 23, transcendentals=0),
    )
    image, differ = call(
        first_kernel,
        (),
        (field, *halo(field), weights),
        (local, local),
        "first_image",
    )
    early, inverse_high, inverse_low = call(
        early_kernel,
        (label,),
        (differ, image, vectors, coarsest_inverse),
        (((32, 128), F32), ((256, 2048), BF16), ((256, 2048), BF16)),
        "early_part",
        pl.CostEstimate(flops=1 << 20, bytes_accessed=1 << 22, transcendentals=0),
    )
    image_two, send = call(
        second_kernel,
        (),
        (differ, *halo(differ), weights, image, vectors, early),
        (local, ((8, 8, 128), F32)),
        "second_image",
    )
    recv = lax.all_to_all(send, BLOCK, 0, 0, tiled=True)
    (send,) = call(gather_kernel, (), (recv,), (((64, 8, 128), F32),), "block_sum")
    recv = lax.all_to_all(send, LATTICE, 0, 0, tiled=True)
    (send,) = call(
        coarse_kernel,
        (),
        (recv, inverse_high, inverse_low),
        (((32, 4, 128), F32),),
        "coarse_solve",
        scratch=[pltpu.VMEM((16, 8, 128), F32)],
    )
    recv = lax.all_to_all(send, COLUMN, 0, 0, tiled=True)
    solved, residual = call(
        last_kernel,
        (),
        (recv, field, differ, image, image_two, vectors),
        (local, local),
        "last_update",
    )
    return solved[None, None, None], residual[None, None, None]


def solution(mesh):
    blocks = Mesh(mesh.devices.reshape(4, 2, 4, 2, 4, 2), ("T", "a", "Z", "b", "Y", "c"))
    spec = P(TA, GZ, XY)
    return jax.shard_map(
        body,
        mesh=blocks,
        in_specs=(spec, spec, spec, spec, P(XY)),
        out_specs=(spec, spec),
        check_vma=False,
    )
```

```python
import jax
import jax.numpy as jnp
from jax import lax
from jax.experimental import pallas as pl
from jax.experimental.pallas import tpu as pltpu
from jax.sharding import Mesh
from jax.sharding import PartitionSpec as P


TA, GZ, XY = ("T", "a"), ("Z", "b"), ("Y", "c")
COLUMN = ("a", "b", "Y", "c")
BLOCK = ("a", "b", "c")
LATTICE = ("T", "Z", "Y")
SIDES = [(XY, 1), (XY, -1), (TA, 1), (TA, -1), (GZ, 1), (GZ, -1)]
OFFSETS = [5, 6, 1, 2, 3, 4]
HIGHEST = lax.Precision.HIGHEST
F32 = jnp.float32
BF16 = jnp.bfloat16
NT = (((1,), (1,)), ((), ()))
NN = (((1,), (0,)), ((), ()))


def dot(left, right, dims):
    return lax.dot_general(left, right, dims, precision=HIGHEST, preferred_element_type=F32)


def split(value):
    high = value.astype(BF16)
    return high, (value - high.astype(F32)).astype(BF16)


def prepare_kernel(stencil, weights):
    rows = lax.broadcasted_iota(jnp.int32, (128, 128), 0)
    cols = lax.broadcasted_iota(jnp.int32, (128, 128), 1)
    unit = jnp.where(rows == cols, 1.0, 0.0).astype(F32)
    for site in range(2):
        for slot in range(8):
            if slot == 0:
                block = stencil[site, 0] - unit
            elif slot == 1:
                block = stencil[site, 7] + stencil[site, 8]
            else:
                block = stencil[site, OFFSETS[slot - 2]]
            high, low = split(jnp.transpose(block))
            start = 128 * (slot % 2)
            weights[site, slot // 2, start : start + 128, 0:128] = high
            weights[site, slot // 2, start : start + 128, 128:256] = low


def change(field, sides, weights, site):
    sides = [field[site], field[1 - site]] + [side[site] for side in sides]
    total = jnp.zeros((64, 256), F32)
    for pair in range(4):
        high, low = split(jnp.concatenate(sides[2 * pair : 2 * pair + 2], axis=1))
        both = jnp.concatenate([high, low], axis=0)
        total = total + lax.dot_general(
            both, weights[site, pair], NN, preferred_element_type=F32
        )
    half = total[0:32] + total[32:64]
    return half[:, 0:128] + half[:, 128:256]


def first_kernel(field, s0, s1, s2, s3, s4, s5, weights, image, differ):
    for site in range(2):
        value = change(field, (s0, s1, s2, s3, s4, s5), weights, site)
        image[site] = field[site] + value
        differ[site] = -value


def padded(vectors, start):
    rows = jnp.concatenate([vectors[0], vectors[1]], axis=1)
    parts = [rows]
    if start:
        parts.insert(0, jnp.zeros((start, 256), F32))
    if start < 96:
        parts.append(jnp.zeros((96 - start, 256), F32))
    return jnp.concatenate(parts, axis=0)


def inner(one, other):
    return jnp.sum(one[0] * other[0] + one[1] * other[1], axis=1, keepdims=True)


def wide(field):
    return jnp.concatenate([field[0], field[1]], axis=1)


def early_kernel(label, differ, image, vectors, inverse, packed, inverse_high, inverse_low):
    lane = lax.broadcasted_iota(jnp.int32, (32, 128), 1)
    value = dot(wide(differ), padded(vectors, 0), NT)
    value = value + dot(wide(image), padded(vectors, 32), NT)
    value = jnp.where(lane == 96, inner(image, image), value)
    value = jnp.where(lane == 97, inner(image, differ), value)
    packed[...] = jnp.where(lane == 101, label[0].astype(F32), value)
    high, low = split(inverse[...])
    inverse_high[...] = high
    inverse_low[...] = low


def second_kernel(
    differ, s0, s1, s2, s3, s4, s5, weights, image, vectors, early, image_two, send
):
    lane = lax.broadcasted_iota(jnp.int32, (32, 128), 1)
    values = []
    for site in range(2):
        value = differ[site] + change(differ, (s0, s1, s2, s3, s4, s5), weights, site)
        image_two[site] = value
        values.append(value)
    packed = early[...] + dot(wide(values), padded(vectors, 64), NT)
    packed = jnp.where(lane == 98, inner(image, values), packed)
    packed = jnp.where(lane == 99, inner(differ, values), packed)
    packed = jnp.where(lane == 100, inner(values, values), packed)
    for group in range(4):
        for c in range(2):
            send[2 * group + c] = packed[8 * group : 8 * group + 8]


def gather_kernel(recv, send):
    total = recv[0]
    for other in range(1, 8):
        total = total + recv[other]
    for other in range(64):
        send[other] = total


def turns(value):
    return [value] + [pltpu.roll(value, 32 * place, 1) for place in range(1, 4)]


def pack(rolled, place, row, lane):
    turned = jnp.zeros((8, 128), F32)
    for right in range(4):
        group = -right % 4
        here = jnp.logical_and(row % 4 == right, lane // 32 == group)
        turned = jnp.where(here, rolled[(group - place) % 4], turned)
    low = jnp.sum(jnp.where(row < 4, turned, 0.0), axis=0, keepdims=True)
    high = jnp.sum(jnp.where(row < 4, 0.0, turned), axis=0, keepdims=True)
    return low, high


def coarse_kernel(recv, inverse_high, inverse_low, send, rows):
    lane = lax.broadcasted_iota(jnp.int32, (8, 128), 1)
    row = lax.broadcasted_iota(jnp.int32, (8, 128), 0)

    def pick(value, place):
        return jnp.sum(jnp.where(lane == place, value, 0.0), axis=1, keepdims=True)

    numbers = []
    for start in range(0, 64, 8):
        tops = jnp.concatenate([recv[start + place, 0:1, :] for place in range(8)], axis=0)
        numbers.append((pick(tops, 101) * 0.125).astype(jnp.int32))
    total = recv[0]
    for source in range(1, 64):
        total = total + recv[source]
    ww, wu, wq, qu, qq = [pick(total, 96 + place) for place in range(5)]
    first = wu / ww
    gamma = wq / ww
    sigma = (qu - gamma * wu) / (qq - gamma * wq)
    kappa = sigma * gamma - first
    group = lane // 32
    for source in range(64):
        number = numbers[source // 8][source % 8, 0]
        part = recv[source]
        mixed = part + kappa * pltpu.roll(part, 96, 1) - sigma * pltpu.roll(part, 64, 1)
        mixed = pltpu.roll(mixed, 32 * (number % 4), 1)
        pltpu.store(rows.at[number // 4], mixed, mask=group == number % 4)
    high, low = split(jnp.concatenate([rows[place] for place in range(16)], axis=1))
    both = jnp.concatenate([high, low], axis=0)
    base = 8 * lax.axis_index(XY)
    own = 16 * lax.axis_index("T") + 4 * lax.axis_index("Z")
    labels = [pick(recv[own + y], 101)[0:1] * 0.125 - base.astype(F32) for y in range(4)]
    turned = jnp.where(lane == row, sigma, jnp.where(lane == row + 8, kappa, 0.0))
    scalars = jnp.sum(turned, axis=0, keepdims=True)
    out = [[jnp.zeros((1, 128), F32) for _ in range(3)] for _ in range(4)]
    for half in range(2):
        begin = 128 * half
        value = lax.dot_general(
            both, inverse_high[begin : begin + 128], NT, preferred_element_type=F32
        )
        value = value[0:8] + value[8:16]
        value = value + lax.dot_general(
            high, inverse_low[begin : begin + 128], NT, preferred_element_type=F32
        )
        rolled = turns(value)
        for place in range(4):
            packed = (*pack(rolled, place, row, lane), scalars)
            for y in range(4):
                for line in range(3):
                    out[y][line] = jnp.where(
                        labels[y] == float(4 * half + place), packed[line], out[y][line]
                    )
    for y in range(4):
        block = jnp.concatenate([*out[y], jnp.zeros((1, 128), F32)], axis=0)
        for side in range(4):
            for c in range(2):
                send[8 * side + 2 * y + c] = block


def last_kernel(recv, field, differ, image, image_two, vectors, solved, residual):
    lane = lax.broadcasted_iota(jnp.int32, (8, 128), 1)
    row = lax.broadcasted_iota(jnp.int32, (8, 128), 0)
    parts, sigmas, kappas = [], [], []
    for group in range(4):
        total = recv[8 * group]
        for other in range(1, 8):
            total = total + recv[8 * group + other]
        lines = jnp.where(row < 4, total[0:1], total[1:2])
        rolled = turns(lines)
        for right in range(1, 4):
            lines = jnp.where(row % 4 == right, rolled[right], lines)
        parts.append(lines)
        scalars = jnp.broadcast_to(total[2:3], (8, 128))
        sigmas.append(jnp.sum(jnp.where(lane == row, scalars, 0.0), axis=1, keepdims=True))
        kappas.append(jnp.sum(jnp.where(lane == row + 8, scalars, 0.0), axis=1, keepdims=True))
    correction = jnp.concatenate(parts, axis=0)[:, 0:32]
    sigma, kappa = jnp.concatenate(sigmas, axis=0), jnp.concatenate(kappas, axis=0)
    for site in range(2):
        b, u, w, q = field[site], differ[site], image[site], image_two[site]
        residual[site] = u + kappa * w - sigma * q
        solved[site] = (1.0 - kappa) * b + sigma * u + dot(correction, vectors[site], NN)


def call(kernel, scalars, arrays, outs, name, cost=None, scratch=()):
    return pl.pallas_call(
        kernel,
        out_shape=[jax.ShapeDtypeStruct(shape, kind) for shape, kind in outs],
        in_specs=[pl.BlockSpec(memory_space=pltpu.SMEM)] * len(scalars)
        + [pl.BlockSpec(memory_space=pltpu.VMEM)] * len(arrays),
        out_specs=[pl.BlockSpec(memory_space=pltpu.VMEM)] * len(outs),
        compiler_params=pltpu.CompilerParams(vmem_limit_bytes=16 * 1024 * 1024),
        cost_estimate=cost,
        scratch_shapes=scratch,
        name=name,
    )(*scalars, *arrays)


def halo(field):
    sides = []
    for axis, step in SIDES:
        sides.append(lax.ppermute(field, axis, [((i + step) % 8, i) for i in range(8)]))
    return sides


def body(right_side, stencil, restrict, aggregate, coarsest_inverse):
    field = right_side[0, 0, 0]
    vectors = restrict[0, 0, 0]
    local = (field.shape, F32)
    label = aggregate.reshape(2)
    (weights,) = call(
        prepare_kernel,
        (),
        (stencil[0, 0, 0],),
        (((2, 4, 256, 256), BF16),),
        "prepare",
        pl.CostEstimate(flops=1 << 20, bytes_accessed=1 << 23, transcendentals=0),
    )
    image, differ = call(
        first_kernel,
        (),
        (field, *halo(field), weights),
        (local, local),
        "first_image",
    )
    early, inverse_high, inverse_low = call(
        early_kernel,
        (label,),
        (differ, image, vectors, coarsest_inverse),
        (((32, 128), F32), ((256, 2048), BF16), ((256, 2048), BF16)),
        "early_part",
        pl.CostEstimate(flops=1 << 20, bytes_accessed=1 << 22, transcendentals=0),
    )
    image_two, send = call(
        second_kernel,
        (),
        (differ, *halo(differ), weights, image, vectors, early),
        (local, ((8, 8, 128), F32)),
        "second_image",
    )
    recv = lax.all_to_all(send, BLOCK, 0, 0, tiled=True)
    (send,) = call(gather_kernel, (), (recv,), (((64, 8, 128), F32),), "block_sum")
    recv = lax.all_to_all(send, LATTICE, 0, 0, tiled=True)
    (send,) = call(
        coarse_kernel,
        (),
        (recv, inverse_high, inverse_low),
        (((32, 4, 128), F32),),
        "coarse_solve",
        scratch=[pltpu.VMEM((16, 8, 128), F32)],
    )
    recv = lax.all_to_all(send, COLUMN, 0, 0, tiled=True)
    solved, residual = call(
        last_kernel,
        (),
        (recv, field, differ, image, image_two, vectors),
        (local, local),
        "last_update",
    )
    return solved[None, None, None], residual[None, None, None]


def solution(mesh):
    blocks = Mesh(mesh.devices.reshape(4, 2, 4, 2, 4, 2), ("T", "a", "Z", "b", "Y", "c"))
    spec = P(TA, GZ, XY)
    return jax.shard_map(
        body,
        mesh=blocks,
        in_specs=(spec, spec, spec, spec, P(XY)),
        out_specs=(spec, spec),
        check_vma=False,
    )
```

```python
import jax
import jax.numpy as jnp
from jax import lax
from jax.experimental import pallas as pl
from jax.experimental.pallas import tpu as pltpu
from jax.sharding import Mesh
from jax.sharding import PartitionSpec as P


TA, GZ, XY = ("T", "a"), ("Z", "b"), ("Y", "c")
COLUMN = ("a", "b", "Y", "c")
BLOCK = ("a", "b", "c")
LATTICE = ("T", "Z", "Y")
SIDES = [(XY, 1), (XY, -1), (TA, 1), (TA, -1), (GZ, 1), (GZ, -1)]
OFFSETS = [5, 6, 1, 2, 3, 4]
HIGHEST = lax.Precision.HIGHEST
F32 = jnp.float32
BF16 = jnp.bfloat16
NT = (((1,), (1,)), ((), ()))
NN = (((1,), (0,)), ((), ()))


def dot(left, right, dims):
    return lax.dot_general(left, right, dims, precision=HIGHEST, preferred_element_type=F32)


def split(value):
    high = value.astype(BF16)
    return high, (value - high.astype(F32)).astype(BF16)


def prepare_kernel(stencil, weights):
    rows = lax.broadcasted_iota(jnp.int32, (128, 128), 0)
    cols = lax.broadcasted_iota(jnp.int32, (128, 128), 1)
    unit = jnp.where(rows == cols, 1.0, 0.0).astype(F32)
    for site in range(2):
        for slot in range(8):
            if slot == 0:
                block = stencil[site, 0] - unit
            elif slot == 1:
                block = stencil[site, 7] + stencil[site, 8]
            else:
                block = stencil[site, OFFSETS[slot - 2]]
            high, low = split(jnp.transpose(block))
            start = 128 * (slot % 2)
            weights[site, slot // 2, start : start + 128, 0:128] = high
            weights[site, slot // 2, start : start + 128, 128:256] = low


def change(field, sides, weights, site):
    sides = [field[site], field[1 - site]] + [side[site] for side in sides]
    return change_from(sides, weights, site)


def change_from(sides, weights, site):
    total = jnp.zeros((64, 256), F32)
    for pair in range(4):
        high, low = split(jnp.concatenate(sides[2 * pair : 2 * pair + 2], axis=1))
        both = jnp.concatenate([high, low], axis=0)
        total = total + lax.dot_general(
            both, weights[site, pair], NN, preferred_element_type=F32
        )
    half = total[0:32] + total[32:64]
    return half[:, 0:128] + half[:, 128:256]


def first_kernel(field, s0, s1, s2, s3, s4, s5, weights, image, differ, send):
    for site in range(2):
        value = change(field, (s0, s1, s2, s3, s4, s5), weights, site)
        image[site] = field[site] + value
        differ[site] = -value
        for other in range(4):
            send[other, site] = -value


def padded(vectors, start):
    rows = jnp.concatenate([vectors[0], vectors[1]], axis=1)
    parts = [rows]
    if start:
        parts.insert(0, jnp.zeros((start, 256), F32))
    if start < 96:
        parts.append(jnp.zeros((96 - start, 256), F32))
    return jnp.concatenate(parts, axis=0)


def inner(one, other):
    return jnp.sum(one[0] * other[0] + one[1] * other[1], axis=1, keepdims=True)


def wide(field):
    return jnp.concatenate([field[0], field[1]], axis=1)


def early_kernel(label, differ, image, vectors, packed):
    lane = lax.broadcasted_iota(jnp.int32, (32, 128), 1)
    value = dot(wide(differ), padded(vectors, 0), NT)
    value = value + dot(wide(image), padded(vectors, 32), NT)
    value = jnp.where(lane == 96, inner(image, image), value)
    value = jnp.where(lane == 97, inner(image, differ), value)
    packed[...] = jnp.where(lane == 101, label[0].astype(F32), value)


def second_kernel(
    differ, near, far, s4, s5, weights, image, vectors, early, image_two, send
):
    a, c = lax.axis_index("a"), lax.axis_index("c")
    one, other = 2 * (1 - a) + c, 2 * a + 1 - c
    near_y, near_z, far_y, far_z = near.at[one], near.at[other], far.at[other], far.at[one]
    lane = lax.broadcasted_iota(jnp.int32, (32, 128), 1)
    values = []
    for site in range(2):
        sides = [
            jnp.where(c == 0, near_z[site], far_z[site]),
            jnp.where(c == 0, far_z[site], near_z[site]),
            jnp.where(a == 0, near_y[site], far_y[site]),
            jnp.where(a == 0, far_y[site], near_y[site]),
            s4[site],
            s5[site],
        ]
        change_here = change_from([differ[site], differ[1 - site], *sides], weights, site)
        value = differ[site] + change_here
        image_two[site] = value
        values.append(value)
    packed = early[...] + dot(wide(values), padded(vectors, 64), NT)
    packed = jnp.where(lane == 98, inner(image, values), packed)
    packed = jnp.where(lane == 99, inner(differ, values), packed)
    packed = jnp.where(lane == 100, inner(values, values), packed)
    for group in range(4):
        for c in range(2):
            send[2 * group + c] = packed[8 * group : 8 * group + 8]


def gather_kernel(recv, send):
    total = recv[0]
    for other in range(1, 8):
        total = total + recv[other]
    for other in range(64):
        send[other] = total


def turns(value):
    return [value] + [pltpu.roll(value, 32 * place, 1) for place in range(1, 4)]


def pack(rolled, place, row, lane):
    turned = jnp.zeros((8, 128), F32)
    for right in range(4):
        group = -right % 4
        here = jnp.logical_and(row % 4 == right, lane // 32 == group)
        turned = jnp.where(here, rolled[(group - place) % 4], turned)
    low = jnp.sum(jnp.where(row < 4, turned, 0.0), axis=0, keepdims=True)
    high = jnp.sum(jnp.where(row < 4, 0.0, turned), axis=0, keepdims=True)
    return low, high


def coarse_kernel(recv, inverse, send, rows):
    lane = lax.broadcasted_iota(jnp.int32, (8, 128), 1)
    row = lax.broadcasted_iota(jnp.int32, (8, 128), 0)

    def pick(value, place):
        return jnp.sum(jnp.where(lane == place, value, 0.0), axis=1, keepdims=True)

    numbers = []
    for start in range(0, 64, 8):
        tops = jnp.concatenate([recv[start + place, 0:1, :] for place in range(8)], axis=0)
        numbers.append((pick(tops, 101) * 0.125).astype(jnp.int32))
    total = recv[0]
    for source in range(1, 64):
        total = total + recv[source]
    ww, wu, wq, qu, qq = [pick(total, 96 + place) for place in range(5)]
    first = wu / ww
    gamma = wq / ww
    sigma = (qu - gamma * wu) / (qq - gamma * wq)
    kappa = sigma * gamma - first
    group = lane // 32
    for source in range(64):
        number = numbers[source // 8][source % 8, 0]
        part = recv[source]
        mixed = part + kappa * pltpu.roll(part, 96, 1) - sigma * pltpu.roll(part, 64, 1)
        mixed = pltpu.roll(mixed, 32 * (number % 4), 1)
        pltpu.store(rows.at[number // 4], mixed, mask=group == number % 4)
    high, low = split(jnp.concatenate([rows[place] for place in range(16)], axis=1))
    both = jnp.concatenate([high, low], axis=0)
    base = 8 * lax.axis_index(XY)
    own = 16 * lax.axis_index("T") + 4 * lax.axis_index("Z")
    labels = [pick(recv[own + y], 101)[0:1] * 0.125 - base.astype(F32) for y in range(4)]
    turned = jnp.where(lane == row, sigma, jnp.where(lane == row + 8, kappa, 0.0))
    scalars = jnp.sum(turned, axis=0, keepdims=True)
    out = [[jnp.zeros((1, 128), F32) for _ in range(3)] for _ in range(4)]
    for half in range(2):
        begin = 128 * half
        held_high, held_low = split(inverse[begin : begin + 128])
        value = lax.dot_general(both, held_high, NT, preferred_element_type=F32)
        value = value[0:8] + value[8:16]
        value = value + lax.dot_general(high, held_low, NT, preferred_element_type=F32)
        rolled = turns(value)
        for place in range(4):
            packed = (*pack(rolled, place, row, lane), scalars)
            for y in range(4):
                for line in range(3):
                    out[y][line] = jnp.where(
                        labels[y] == float(4 * half + place), packed[line], out[y][line]
                    )
    for y in range(4):
        block = jnp.concatenate([*out[y], jnp.zeros((1, 128), F32)], axis=0)
        for side in range(4):
            for c in range(2):
                send[8 * side + 2 * y + c] = block


def last_kernel(recv, field, differ, image, image_two, vectors, solved, residual):
    lane = lax.broadcasted_iota(jnp.int32, (8, 128), 1)
    row = lax.broadcasted_iota(jnp.int32, (8, 128), 0)
    parts, sigmas, kappas = [], [], []
    for group in range(4):
        total = recv[8 * group]
        for other in range(1, 8):
            total = total + recv[8 * group + other]
        lines = jnp.where(row < 4, total[0:1], total[1:2])
        rolled = turns(lines)
        for right in range(1, 4):
            lines = jnp.where(row % 4 == right, rolled[right], lines)
        parts.append(lines)
        scalars = jnp.broadcast_to(total[2:3], (8, 128))
        sigmas.append(jnp.sum(jnp.where(lane == row, scalars, 0.0), axis=1, keepdims=True))
        kappas.append(jnp.sum(jnp.where(lane == row + 8, scalars, 0.0), axis=1, keepdims=True))
    correction = jnp.concatenate(parts, axis=0)[:, 0:32]
    sigma, kappa = jnp.concatenate(sigmas, axis=0), jnp.concatenate(kappas, axis=0)
    for site in range(2):
        b, u, w, q = field[site], differ[site], image[site], image_two[site]
        residual[site] = u + kappa * w - sigma * q
        solved[site] = (1.0 - kappa) * b + sigma * u + dot(correction, vectors[site], NN)


def call(kernel, scalars, arrays, outs, name, cost=None, scratch=()):
    return pl.pallas_call(
        kernel,
        out_shape=[jax.ShapeDtypeStruct(shape, kind) for shape, kind in outs],
        in_specs=[pl.BlockSpec(memory_space=pltpu.SMEM)] * len(scalars)
        + [pl.BlockSpec(memory_space=pltpu.VMEM)] * len(arrays),
        out_specs=[pl.BlockSpec(memory_space=pltpu.VMEM)] * len(outs),
        compiler_params=pltpu.CompilerParams(vmem_limit_bytes=16 * 1024 * 1024),
        cost_estimate=cost,
        scratch_shapes=scratch,
        name=name,
    )(*scalars, *arrays)


def halo(field):
    sides = []
    for axis, step in SIDES:
        sides.append(lax.ppermute(field, axis, [((i + step) % 8, i) for i in range(8)]))
    return sides


def quads():
    groups = []
    for first in range(4):
        for z in range(8):
            for last in range(4):
                groups.append(
                    [
                        (2 * first + a + 1) % 8 * 64 + z * 8 + (2 * last + c + 1) % 8
                        for a in range(2)
                        for c in range(2)
                    ]
                )
    return groups


def quad_halo(field, send):
    sides = []
    for axis, step in SIDES[4:]:
        sides.append(lax.ppermute(field, axis, [((i + step) % 8, i) for i in range(8)]))
    near = lax.all_to_all(send, ("a", "c"), 0, 0, tiled=True)
    far = lax.all_to_all(send, TA + GZ + XY, 0, 0, tiled=True, axis_index_groups=quads())
    return near, far, *sides


def body(right_side, stencil, restrict, aggregate, coarsest_inverse):
    field = right_side[0, 0, 0]
    vectors = restrict[0, 0, 0]
    local = (field.shape, F32)
    label = aggregate.reshape(2)
    (weights,) = call(
        prepare_kernel,
        (),
        (stencil[0, 0, 0],),
        (((2, 4, 256, 256), BF16),),
        "prepare",
        pl.CostEstimate(flops=1 << 20, bytes_accessed=1 << 23, transcendentals=0),
    )
    image, differ, copies = call(
        first_kernel,
        (),
        (field, *halo(field), weights),
        (local, local, ((4, *field.shape), F32)),
        "first_image",
    )
    (early,) = call(
        early_kernel, (label,), (differ, image, vectors), (((32, 128), F32),), "early_part"
    )
    image_two, send = call(
        second_kernel,
        (),
        (differ, *quad_halo(differ, copies), weights, image, vectors, early),
        (local, ((8, 8, 128), F32)),
        "second_image",
    )
    recv = lax.all_to_all(send, BLOCK, 0, 0, tiled=True)
    (send,) = call(gather_kernel, (), (recv,), (((64, 8, 128), F32),), "block_sum")
    recv = lax.all_to_all(send, LATTICE, 0, 0, tiled=True)
    (send,) = call(
        coarse_kernel,
        (),
        (recv, coarsest_inverse),
        (((32, 4, 128), F32),),
        "coarse_solve",
        scratch=[pltpu.VMEM((16, 8, 128), F32)],
    )
    recv = lax.all_to_all(send, COLUMN, 0, 0, tiled=True)
    solved, residual = call(
        last_kernel,
        (),
        (recv, field, differ, image, image_two, vectors),
        (local, local),
        "last_update",
    )
    return solved[None, None, None], residual[None, None, None]


def solution(mesh):
    blocks = Mesh(mesh.devices.reshape(4, 2, 4, 2, 4, 2), ("T", "a", "Z", "b", "Y", "c"))
    spec = P(TA, GZ, XY)
    return jax.shard_map(
        body,
        mesh=blocks,
        in_specs=(spec, spec, spec, spec, P(XY)),
        out_specs=(spec, spec),
        check_vma=False,
    )
```

```python
import jax
import jax.numpy as jnp
from jax import lax
from jax.experimental import pallas as pl
from jax.experimental.pallas import tpu as pltpu
from jax.sharding import Mesh
from jax.sharding import PartitionSpec as P


TA, GZ, XY = ("T", "a"), ("Z", "b"), ("Y", "c")
COLUMN = ("a", "b", "Y", "c")
PLANE = ("T", "Z")
SIDES = [(GZ, 1), (TA, 1), (XY, 1), (GZ, -1), (TA, -1), (XY, -1)]
OFFSETS = [3, 1, 5, 4, 2, 6]
HIGHEST = lax.Precision.HIGHEST
F32 = jnp.float32
BF16 = jnp.bfloat16
NT = (((1,), (1,)), ((), ()))
NN = (((1,), (0,)), ((), ()))


def dot(left, right, dims):
    return lax.dot_general(left, right, dims, precision=HIGHEST, preferred_element_type=F32)


def split(value):
    high = value.astype(BF16)
    return high, (value - high.astype(F32)).astype(BF16)


def prepare_kernel(stencil, weights):
    rows = lax.broadcasted_iota(jnp.int32, (128, 128), 0)
    cols = lax.broadcasted_iota(jnp.int32, (128, 128), 1)
    unit = jnp.where(rows == cols, 1.0, 0.0).astype(F32)
    for site in range(2):
        for slot in range(8):
            if slot == 0:
                block = stencil[site, 0] - unit
            elif slot == 1:
                block = stencil[site, 7] + stencil[site, 8]
            else:
                block = stencil[site, OFFSETS[slot - 2]]
            high, low = split(jnp.transpose(block))
            start = 128 * (slot % 2)
            weights[site, slot // 2, start : start + 128, 0:128] = high
            weights[site, slot // 2, start : start + 128, 128:256] = low


def change(field, sides, weights, site):
    sides = [field[site], field[1 - site]] + [side[site] for side in sides]
    total = jnp.zeros((64, 256), F32)
    for pair in range(4):
        high, low = split(jnp.concatenate(sides[2 * pair : 2 * pair + 2], axis=1))
        both = jnp.concatenate([high, low], axis=0)
        total = total + lax.dot_general(
            both, weights[site, pair], NN, preferred_element_type=F32
        )
    half = total[0:32] + total[32:64]
    return half[:, 0:128] + half[:, 128:256]


def first_kernel(field, s0, s1, s2, s3, s4, s5, weights, image, differ):
    for site in range(2):
        value = change(field, (s0, s1, s2, s3, s4, s5), weights, site)
        image[site] = field[site] + value
        differ[site] = -value


def padded(vectors, start):
    rows = jnp.concatenate([vectors[0], vectors[1]], axis=1)
    parts = [rows]
    if start:
        parts.insert(0, jnp.zeros((start, 256), F32))
    if start < 96:
        parts.append(jnp.zeros((96 - start, 256), F32))
    return jnp.concatenate(parts, axis=0)


def inner(one, other):
    return jnp.sum(one[0] * other[0] + one[1] * other[1], axis=1, keepdims=True)


def wide(field):
    return jnp.concatenate([field[0], field[1]], axis=1)


def early_kernel(label, differ, image, vectors, packed):
    lane = lax.broadcasted_iota(jnp.int32, (32, 128), 1)
    value = dot(wide(differ), padded(vectors, 0), NT)
    value = value + dot(wide(image), padded(vectors, 32), NT)
    value = jnp.where(lane == 96, inner(image, image), value)
    value = jnp.where(lane == 97, inner(image, differ), value)
    packed[...] = jnp.where(lane == 101, label[0].astype(F32), value)


def second_kernel(
    differ, s0, s1, s2, s3, s4, s5, weights, image, vectors, early, image_two, send
):
    lane = lax.broadcasted_iota(jnp.int32, (32, 128), 1)
    values = []
    for site in range(2):
        value = differ[site] + change(differ, (s0, s1, s2, s3, s4, s5), weights, site)
        image_two[site] = value
        values.append(value)
    packed = early[...] + dot(wide(values), padded(vectors, 64), NT)
    packed = jnp.where(lane == 98, inner(image, values), packed)
    packed = jnp.where(lane == 99, inner(differ, values), packed)
    packed = jnp.where(lane == 100, inner(values, values), packed)
    for group in range(4):
        for other in range(8):
            send[8 * group + other] = packed[8 * group : 8 * group + 8]


def gather_kernel(recv, send):
    for y in range(4):
        total = recv[2 * y] + recv[2 * y + 1]
        for side in range(1, 4):
            total = total + (recv[8 * side + 2 * y] + recv[8 * side + 2 * y + 1])
        for other in range(16):
            send[other, y] = total


def turns(value):
    return [value] + [pltpu.roll(value, 32 * place, 1) for place in range(1, 4)]


def pack(rolled, place, row, lane):
    turned = jnp.zeros((8, 128), F32)
    for right in range(4):
        group = -right % 4
        here = jnp.logical_and(row % 4 == right, lane // 32 == group)
        turned = jnp.where(here, rolled[(group - place) % 4], turned)
    low = jnp.sum(jnp.where(row < 4, turned, 0.0), axis=0, keepdims=True)
    high = jnp.sum(jnp.where(row < 4, 0.0, turned), axis=0, keepdims=True)
    return low, high


def coarse_kernel(recv, inverse, send, rows):
    lane = lax.broadcasted_iota(jnp.int32, (8, 128), 1)
    row = lax.broadcasted_iota(jnp.int32, (8, 128), 0)

    def pick(value, place):
        return jnp.sum(jnp.where(lane == place, value, 0.0), axis=1, keepdims=True)

    numbers = []
    for start in range(0, 64, 8):
        tops = jnp.concatenate([recv[start + place, 0:1, :] for place in range(8)], axis=0)
        numbers.append((pick(tops, 101) * 0.125).astype(jnp.int32))
    total = recv[0]
    for source in range(1, 64):
        total = total + recv[source]
    ww, wu, wq, qu, qq = [pick(total, 96 + place) for place in range(5)]
    first = wu / ww
    gamma = wq / ww
    sigma = (qu - gamma * wu) / (qq - gamma * wq)
    kappa = sigma * gamma - first
    group = lane // 32
    for source in range(64):
        number = numbers[source // 8][source % 8, 0]
        part = recv[source]
        mixed = part + kappa * pltpu.roll(part, 96, 1) - sigma * pltpu.roll(part, 64, 1)
        mixed = pltpu.roll(mixed, 32 * (number % 4), 1)
        pltpu.store(rows.at[number // 4], mixed, mask=group == number % 4)
    high, low = split(jnp.concatenate([rows[place] for place in range(16)], axis=1))
    both = jnp.concatenate([high, low], axis=0)
    base = 8 * lax.axis_index(XY)
    own = 16 * lax.axis_index("T") + 4 * lax.axis_index("Z")
    labels = [pick(recv[own + y], 101)[0:1] * 0.125 - base.astype(F32) for y in range(4)]
    turned = jnp.where(lane == row, sigma, jnp.where(lane == row + 8, kappa, 0.0))
    scalars = jnp.sum(turned, axis=0, keepdims=True)
    out = [[jnp.zeros((1, 128), F32) for _ in range(3)] for _ in range(4)]
    for half in range(2):
        begin = 128 * half
        held_high, held_low = split(inverse[begin : begin + 128])
        value = lax.dot_general(both, held_high, NT, preferred_element_type=F32)
        value = value[0:8] + value[8:16]
        value = value + lax.dot_general(high, held_low, NT, preferred_element_type=F32)
        rolled = turns(value)
        for place in range(4):
            packed = (*pack(rolled, place, row, lane), scalars)
            for y in range(4):
                for line in range(3):
                    out[y][line] = jnp.where(
                        labels[y] == float(4 * half + place), packed[line], out[y][line]
                    )
    for y in range(4):
        block = jnp.concatenate([*out[y], jnp.zeros((1, 128), F32)], axis=0)
        for side in range(4):
            for c in range(2):
                send[8 * side + 2 * y + c] = block


def last_kernel(recv, field, differ, image, image_two, vectors, solved, residual):
    lane = lax.broadcasted_iota(jnp.int32, (8, 128), 1)
    row = lax.broadcasted_iota(jnp.int32, (8, 128), 0)
    parts, sigmas, kappas = [], [], []
    for group in range(4):
        total = recv[8 * group]
        for other in range(1, 8):
            total = total + recv[8 * group + other]
        lines = jnp.where(row < 4, total[0:1], total[1:2])
        rolled = turns(lines)
        for right in range(1, 4):
            lines = jnp.where(row % 4 == right, rolled[right], lines)
        parts.append(lines)
        scalars = jnp.broadcast_to(total[2:3], (8, 128))
        sigmas.append(jnp.sum(jnp.where(lane == row, scalars, 0.0), axis=1, keepdims=True))
        kappas.append(jnp.sum(jnp.where(lane == row + 8, scalars, 0.0), axis=1, keepdims=True))
    correction = jnp.concatenate(parts, axis=0)[:, 0:32]
    sigma, kappa = jnp.concatenate(sigmas, axis=0), jnp.concatenate(kappas, axis=0)
    for site in range(2):
        b, u, w, q = field[site], differ[site], image[site], image_two[site]
        residual[site] = u + kappa * w - sigma * q
        solved[site] = (1.0 - kappa) * b + sigma * u + dot(correction, vectors[site], NN)


def call(kernel, scalars, arrays, outs, name, cost=None, scratch=()):
    return pl.pallas_call(
        kernel,
        out_shape=[jax.ShapeDtypeStruct(shape, kind) for shape, kind in outs],
        in_specs=[pl.BlockSpec(memory_space=pltpu.SMEM)] * len(scalars)
        + [pl.BlockSpec(memory_space=pltpu.VMEM)] * len(arrays),
        out_specs=[pl.BlockSpec(memory_space=pltpu.VMEM)] * len(outs),
        compiler_params=pltpu.CompilerParams(vmem_limit_bytes=16 * 1024 * 1024),
        cost_estimate=cost,
        scratch_shapes=scratch,
        name=name,
    )(*scalars, *arrays)


def halo(field):
    sides = []
    for axis, step in SIDES:
        sides.append(lax.ppermute(field, axis, [((i + step) % 8, i) for i in range(8)]))
    return sides


def body(right_side, stencil, restrict, aggregate, coarsest_inverse):
    field = right_side[0, 0, 0]
    vectors = restrict[0, 0, 0]
    local = (field.shape, F32)
    label = aggregate.reshape(2)
    (weights,) = call(
        prepare_kernel,
        (),
        (stencil[0, 0, 0],),
        (((2, 4, 256, 256), BF16),),
        "prepare",
        pl.CostEstimate(flops=1 << 20, bytes_accessed=1 << 23, transcendentals=0),
    )
    image, differ = call(
        first_kernel,
        (),
        (field, *halo(field), weights),
        (local, local),
        "first_image",
    )
    (early,) = call(
        early_kernel, (label,), (differ, image, vectors), (((32, 128), F32),), "early_part"
    )
    image_two, send = call(
        second_kernel,
        (),
        (differ, *halo(differ), weights, image, vectors, early),
        (local, ((32, 8, 128), F32)),
        "second_image",
    )
    recv = lax.all_to_all(send, COLUMN, 0, 0, tiled=True)
    (send,) = call(gather_kernel, (), (recv,), (((16, 4, 8, 128), F32),), "block_sum")
    recv = lax.all_to_all(send, PLANE, 0, 0, tiled=True).reshape(64, 8, 128)
    (send,) = call(
        coarse_kernel,
        (),
        (recv, coarsest_inverse),
        (((32, 4, 128), F32),),
        "coarse_solve",
        scratch=[pltpu.VMEM((16, 8, 128), F32)],
    )
    recv = lax.all_to_all(send, COLUMN, 0, 0, tiled=True)
    solved, residual = call(
        last_kernel,
        (),
        (recv, field, differ, image, image_two, vectors),
        (local, local),
        "last_update",
    )
    return solved[None, None, None], residual[None, None, None]


def solution(mesh):
    blocks = Mesh(mesh.devices.reshape(4, 2, 4, 2, 4, 2), ("T", "a", "Z", "b", "Y", "c"))
    spec = P(TA, GZ, XY)
    return jax.shard_map(
        body,
        mesh=blocks,
        in_specs=(spec, spec, spec, spec, P(XY)),
        out_specs=(spec, spec),
        check_vma=False,
    )
```

```python
import jax
import jax.numpy as jnp
from jax import lax
from jax.experimental import pallas as pl
from jax.experimental.pallas import tpu as pltpu
from jax.sharding import Mesh
from jax.sharding import PartitionSpec as P


TA, GZ, XY = ("T", "a"), ("Z", "b"), ("Y", "c")
COLUMN = ("a", "b", "Y", "c")
PLANE = ("T", "Z")
SIDES = [(TA, 1), (TA, -1), (GZ, 1), (GZ, -1), (XY, 1), (XY, -1)]
OFFSETS = [1, 2, 3, 4, 5, 6]
HIGHEST = lax.Precision.HIGHEST
F32 = jnp.float32
BF16 = jnp.bfloat16
NT = (((1,), (1,)), ((), ()))
NN = (((1,), (0,)), ((), ()))


def dot(left, right, dims):
    return lax.dot_general(left, right, dims, precision=HIGHEST, preferred_element_type=F32)


def split(value):
    high = value.astype(BF16)
    return high, (value - high.astype(F32)).astype(BF16)


def prepare_kernel(stencil, weights):
    rows = lax.broadcasted_iota(jnp.int32, (128, 128), 0)
    cols = lax.broadcasted_iota(jnp.int32, (128, 128), 1)
    unit = jnp.where(rows == cols, 1.0, 0.0).astype(F32)
    for site in range(2):
        for slot in range(8):
            if slot == 0:
                block = stencil[site, 0] - unit
            elif slot == 1:
                block = stencil[site, 7] + stencil[site, 8]
            else:
                block = stencil[site, OFFSETS[slot - 2]]
            high, low = split(jnp.transpose(block))
            start = 128 * (slot % 2)
            weights[site, slot // 2, start : start + 128, 0:128] = high
            weights[site, slot // 2, start : start + 128, 128:256] = low


def change(field, sides, weights, site):
    sides = [field[site], field[1 - site]] + [side[site] for side in sides]
    total = jnp.zeros((64, 256), F32)
    for pair in range(4):
        high, low = split(jnp.concatenate(sides[2 * pair : 2 * pair + 2], axis=1))
        both = jnp.concatenate([high, low], axis=0)
        total = total + lax.dot_general(
            both, weights[site, pair], NN, preferred_element_type=F32
        )
    half = total[0:32] + total[32:64]
    return half[:, 0:128] + half[:, 128:256]


def first_kernel(field, s0, s1, s2, s3, s4, s5, weights, image, differ):
    for site in range(2):
        value = change(field, (s0, s1, s2, s3, s4, s5), weights, site)
        image[site] = field[site] + value
        differ[site] = -value


def padded(vectors, start):
    rows = jnp.concatenate([vectors[0], vectors[1]], axis=1)
    parts = [rows]
    if start:
        parts.insert(0, jnp.zeros((start, 256), F32))
    if start < 96:
        parts.append(jnp.zeros((96 - start, 256), F32))
    return jnp.concatenate(parts, axis=0)


def inner(one, other):
    return jnp.sum(one[0] * other[0] + one[1] * other[1], axis=1, keepdims=True)


def wide(field):
    return jnp.concatenate([field[0], field[1]], axis=1)


def early_kernel(label, differ, image, vectors, packed):
    lane = lax.broadcasted_iota(jnp.int32, (32, 128), 1)
    value = dot(wide(differ), padded(vectors, 0), NT)
    value = value + dot(wide(image), padded(vectors, 32), NT)
    value = jnp.where(lane == 96, inner(image, image), value)
    value = jnp.where(lane == 97, inner(image, differ), value)
    packed[...] = jnp.where(lane == 101, label[0].astype(F32), value)


def second_kernel(
    differ, s0, s1, s2, s3, s4, s5, weights, image, vectors, early, image_two, send
):
    lane = lax.broadcasted_iota(jnp.int32, (32, 128), 1)
    values = []
    for site in range(2):
        value = differ[site] + change(differ, (s0, s1, s2, s3, s4, s5), weights, site)
        image_two[site] = value
        values.append(value)
    packed = early[...] + dot(wide(values), padded(vectors, 64), NT)
    packed = jnp.where(lane == 98, inner(image, values), packed)
    packed = jnp.where(lane == 99, inner(differ, values), packed)
    packed = jnp.where(lane == 100, inner(values, values), packed)
    for group in range(4):
        for other in range(8):
            send[8 * group + other] = packed[8 * group : 8 * group + 8]


def gather_kernel(recv, send):
    for y in range(4):
        total = recv[2 * y] + recv[2 * y + 1]
        for side in range(1, 4):
            total = total + (recv[8 * side + 2 * y] + recv[8 * side + 2 * y + 1])
        for other in range(16):
            send[other, y] = total


def turns(value):
    return [value] + [pltpu.roll(value, 32 * place, 1) for place in range(1, 4)]


def pack(rolled, place, row, lane):
    turned = jnp.zeros((8, 128), F32)
    for right in range(4):
        group = -right % 4
        here = jnp.logical_and(row % 4 == right, lane // 32 == group)
        turned = jnp.where(here, rolled[(group - place) % 4], turned)
    low = jnp.sum(jnp.where(row < 4, turned, 0.0), axis=0, keepdims=True)
    high = jnp.sum(jnp.where(row < 4, 0.0, turned), axis=0, keepdims=True)
    return low, high


def coarse_kernel(recv, inverse, send, rows):
    lane = lax.broadcasted_iota(jnp.int32, (8, 128), 1)
    row = lax.broadcasted_iota(jnp.int32, (8, 128), 0)

    def pick(value, place):
        return jnp.sum(jnp.where(lane == place, value, 0.0), axis=1, keepdims=True)

    numbers = []
    for start in range(0, 64, 8):
        tops = jnp.concatenate([recv[start + place, 0:1, :] for place in range(8)], axis=0)
        numbers.append((pick(tops, 101) * 0.125).astype(jnp.int32))
    total = recv[0]
    for source in range(1, 64):
        total = total + recv[source]
    ww, wu, wq, qu, qq = [pick(total, 96 + place) for place in range(5)]
    first = wu / ww
    gamma = wq / ww
    sigma = (qu - gamma * wu) / (qq - gamma * wq)
    kappa = sigma * gamma - first
    group = lane // 32
    for source in range(64):
        number = numbers[source // 8][source % 8, 0]
        part = recv[source]
        mixed = part + kappa * pltpu.roll(part, 96, 1) - sigma * pltpu.roll(part, 64, 1)
        mixed = pltpu.roll(mixed, 32 * (number % 4), 1)
        pltpu.store(rows.at[number // 4], mixed, mask=group == number % 4)
    high, low = split(jnp.concatenate([rows[place] for place in range(16)], axis=1))
    both = jnp.concatenate([high, low], axis=0)
    base = 8 * lax.axis_index(XY)
    own = 16 * lax.axis_index("T") + 4 * lax.axis_index("Z")
    labels = [pick(recv[own + y], 101)[0:1] * 0.125 - base.astype(F32) for y in range(4)]
    turned = jnp.where(lane == row, sigma, jnp.where(lane == row + 8, kappa, 0.0))
    scalars = jnp.sum(turned, axis=0, keepdims=True)
    out = [[jnp.zeros((1, 128), F32) for _ in range(3)] for _ in range(4)]
    for half in range(2):
        begin = 128 * half
        held_high, held_low = split(inverse[begin : begin + 128])
        value = lax.dot_general(both, held_high, NT, preferred_element_type=F32)
        value = value[0:8] + value[8:16]
        value = value + lax.dot_general(high, held_low, NT, preferred_element_type=F32)
        rolled = turns(value)
        for place in range(4):
            packed = (*pack(rolled, place, row, lane), scalars)
            for y in range(4):
                for line in range(3):
                    out[y][line] = jnp.where(
                        labels[y] == float(4 * half + place), packed[line], out[y][line]
                    )
    for y in range(4):
        block = jnp.concatenate([*out[y], jnp.zeros((1, 128), F32)], axis=0)
        for side in range(4):
            for c in range(2):
                send[8 * side + 2 * y + c] = block


def last_kernel(recv, field, differ, image, image_two, vectors, solved, residual):
    lane = lax.broadcasted_iota(jnp.int32, (8, 128), 1)
    row = lax.broadcasted_iota(jnp.int32, (8, 128), 0)
    parts, sigmas, kappas = [], [], []
    for group in range(4):
        total = recv[8 * group]
        for other in range(1, 8):
            total = total + recv[8 * group + other]
        lines = jnp.where(row < 4, total[0:1], total[1:2])
        rolled = turns(lines)
        for right in range(1, 4):
            lines = jnp.where(row % 4 == right, rolled[right], lines)
        parts.append(lines)
        scalars = jnp.broadcast_to(total[2:3], (8, 128))
        sigmas.append(jnp.sum(jnp.where(lane == row, scalars, 0.0), axis=1, keepdims=True))
        kappas.append(jnp.sum(jnp.where(lane == row + 8, scalars, 0.0), axis=1, keepdims=True))
    correction = jnp.concatenate(parts, axis=0)[:, 0:32]
    sigma, kappa = jnp.concatenate(sigmas, axis=0), jnp.concatenate(kappas, axis=0)
    for site in range(2):
        b, u, w, q = field[site], differ[site], image[site], image_two[site]
        residual[site] = u + kappa * w - sigma * q
        solved[site] = (1.0 - kappa) * b + sigma * u + dot(correction, vectors[site], NN)


def call(kernel, scalars, arrays, outs, name, cost=None, scratch=()):
    return pl.pallas_call(
        kernel,
        out_shape=[jax.ShapeDtypeStruct(shape, kind) for shape, kind in outs],
        in_specs=[pl.BlockSpec(memory_space=pltpu.SMEM)] * len(scalars)
        + [pl.BlockSpec(memory_space=pltpu.VMEM)] * len(arrays),
        out_specs=[pl.BlockSpec(memory_space=pltpu.VMEM)] * len(outs),
        compiler_params=pltpu.CompilerParams(vmem_limit_bytes=16 * 1024 * 1024),
        cost_estimate=cost,
        scratch_shapes=scratch,
        name=name,
    )(*scalars, *arrays)


def halo(field):
    sides = []
    for axis, step in SIDES:
        sides.append(lax.ppermute(field, axis, [((i + step) % 8, i) for i in range(8)]))
    return sides


def body(right_side, stencil, restrict, aggregate, coarsest_inverse):
    field = right_side[0, 0, 0]
    vectors = restrict[0, 0, 0]
    local = (field.shape, F32)
    label = aggregate.reshape(2)
    (weights,) = call(
        prepare_kernel,
        (),
        (stencil[0, 0, 0],),
        (((2, 4, 256, 256), BF16),),
        "prepare",
        pl.CostEstimate(flops=1 << 20, bytes_accessed=1 << 23, transcendentals=0),
    )
    image, differ = call(
        first_kernel,
        (),
        (field, *halo(field), weights),
        (local, local),
        "first_image",
    )
    (early,) = call(
        early_kernel, (label,), (differ, image, vectors), (((32, 128), F32),), "early_part"
    )
    image_two, send = call(
        second_kernel,
        (),
        (differ, *halo(differ), weights, image, vectors, early),
        (local, ((32, 8, 128), F32)),
        "second_image",
    )
    recv = lax.all_to_all(send, COLUMN, 0, 0, tiled=True)
    (send,) = call(gather_kernel, (), (recv,), (((16, 4, 8, 128), F32),), "block_sum")
    recv = lax.all_to_all(send, PLANE, 0, 0, tiled=True).reshape(64, 8, 128)
    (send,) = call(
        coarse_kernel,
        (),
        (recv, coarsest_inverse),
        (((32, 4, 128), F32),),
        "coarse_solve",
        scratch=[pltpu.VMEM((16, 8, 128), F32)],
    )
    recv = lax.all_to_all(send, COLUMN, 0, 0, tiled=True)
    solved, residual = call(
        last_kernel,
        (),
        (recv, field, differ, image, image_two, vectors),
        (local, local),
        "last_update",
    )
    return solved[None, None, None], residual[None, None, None]


def solution(mesh):
    blocks = Mesh(mesh.devices.reshape(4, 2, 4, 2, 4, 2), ("T", "a", "Z", "b", "Y", "c"))
    spec = P(TA, GZ, XY)
    return jax.shard_map(
        body,
        mesh=blocks,
        in_specs=(spec, spec, spec, spec, P(XY)),
        out_specs=(spec, spec),
        check_vma=False,
    )
```

```python
import jax
import jax.numpy as jnp
from jax import lax
from jax.experimental import pallas as pl
from jax.experimental.pallas import tpu as pltpu
from jax.sharding import Mesh
from jax.sharding import PartitionSpec as P


TA, GZ, XY = ("T", "a"), ("Z", "b"), ("Y", "c")
COLUMN = ("a", "b", "Y", "c")
BLOCK = ("a", "b", "c")
LATTICE = ("T", "Z", "Y")
SIDES = [(TA, 1), (TA, -1), (GZ, 1), (GZ, -1), (XY, 1), (XY, -1)]
OFFSETS = [1, 2, 3, 4, 5, 6]
HIGHEST = lax.Precision.HIGHEST
F32 = jnp.float32
BF16 = jnp.bfloat16
NT = (((1,), (1,)), ((), ()))
NN = (((1,), (0,)), ((), ()))


def dot(left, right, dims):
    return lax.dot_general(left, right, dims, precision=HIGHEST, preferred_element_type=F32)


def split(value):
    high = value.astype(BF16)
    return high, (value - high.astype(F32)).astype(BF16)


def prepare_kernel(stencil, weights):
    rows = lax.broadcasted_iota(jnp.int32, (128, 128), 0)
    cols = lax.broadcasted_iota(jnp.int32, (128, 128), 1)
    unit = jnp.where(rows == cols, 1.0, 0.0).astype(F32)
    for site in range(2):
        for slot in range(8):
            if slot == 0:
                block = stencil[site, 0] - unit
            elif slot == 1:
                block = stencil[site, 7] + stencil[site, 8]
            else:
                block = stencil[site, OFFSETS[slot - 2]]
            high, low = split(jnp.transpose(block))
            start = 128 * (slot % 2)
            weights[site, slot // 2, start : start + 128, 0:128] = high
            weights[site, slot // 2, start : start + 128, 128:256] = low


def change(field, sides, weights, site):
    sides = [field[site], field[1 - site]] + [side[site] for side in sides]
    total = jnp.zeros((64, 256), F32)
    for pair in range(4):
        high, low = split(jnp.concatenate(sides[2 * pair : 2 * pair + 2], axis=1))
        both = jnp.concatenate([high, low], axis=0)
        total = total + lax.dot_general(
            both, weights[site, pair], NN, preferred_element_type=F32
        )
    half = total[0:32] + total[32:64]
    return half[:, 0:128] + half[:, 128:256]


def first_kernel(field, s0, s1, s2, s3, s4, s5, weights, image, differ):
    for site in range(2):
        value = change(field, (s0, s1, s2, s3, s4, s5), weights, site)
        image[site] = field[site] + value
        differ[site] = -value


def padded(vectors, start):
    rows = jnp.concatenate([vectors[0], vectors[1]], axis=1)
    parts = [rows]
    if start:
        parts.insert(0, jnp.zeros((start, 256), F32))
    if start < 96:
        parts.append(jnp.zeros((96 - start, 256), F32))
    return jnp.concatenate(parts, axis=0)


def inner(one, other):
    return jnp.sum(one[0] * other[0] + one[1] * other[1], axis=1, keepdims=True)


def wide(field):
    return jnp.concatenate([field[0], field[1]], axis=1)


def early_kernel(label, differ, image, vectors, packed):
    lane = lax.broadcasted_iota(jnp.int32, (32, 128), 1)
    value = dot(wide(differ), padded(vectors, 0), NT)
    value = value + dot(wide(image), padded(vectors, 32), NT)
    value = jnp.where(lane == 96, inner(image, image), value)
    value = jnp.where(lane == 97, inner(image, differ), value)
    packed[...] = jnp.where(lane == 101, label[0].astype(F32), value)


def second_kernel(
    differ, s0, s1, s2, s3, s4, s5, weights, image, vectors, early, image_two, send
):
    lane = lax.broadcasted_iota(jnp.int32, (32, 128), 1)
    values = []
    for site in range(2):
        value = differ[site] + change(differ, (s0, s1, s2, s3, s4, s5), weights, site)
        image_two[site] = value
        values.append(value)
    packed = early[...] + dot(wide(values), padded(vectors, 64), NT)
    packed = jnp.where(lane == 98, inner(image, values), packed)
    packed = jnp.where(lane == 99, inner(differ, values), packed)
    packed = jnp.where(lane == 100, inner(values, values), packed)
    for group in range(4):
        for c in range(2):
            send[2 * group + c] = packed[8 * group : 8 * group + 8]


def gather_kernel(recv, send):
    total = recv[0]
    for other in range(1, 8):
        total = total + recv[other]
    for other in range(64):
        send[other] = total


def turns(value):
    return [value] + [pltpu.roll(value, 32 * place, 1) for place in range(1, 4)]


def pack(rolled, place, row, lane):
    turned = jnp.zeros((8, 128), F32)
    for right in range(4):
        group = -right % 4
        here = jnp.logical_and(row % 4 == right, lane // 32 == group)
        turned = jnp.where(here, rolled[(group - place) % 4], turned)
    low = jnp.sum(jnp.where(row < 4, turned, 0.0), axis=0, keepdims=True)
    high = jnp.sum(jnp.where(row < 4, 0.0, turned), axis=0, keepdims=True)
    return low, high


def coarse_kernel(recv, inverse, send, rows):
    lane = lax.broadcasted_iota(jnp.int32, (8, 128), 1)
    row = lax.broadcasted_iota(jnp.int32, (8, 128), 0)

    def pick(value, place):
        return jnp.sum(jnp.where(lane == place, value, 0.0), axis=1, keepdims=True)

    numbers = []
    for start in range(0, 64, 8):
        tops = jnp.concatenate([recv[start + place, 0:1, :] for place in range(8)], axis=0)
        numbers.append((pick(tops, 101) * 0.125).astype(jnp.int32))
    total = recv[0]
    for source in range(1, 64):
        total = total + recv[source]
    ww, wu, wq, qu, qq = [pick(total, 96 + place) for place in range(5)]
    first = wu / ww
    gamma = wq / ww
    sigma = (qu - gamma * wu) / (qq - gamma * wq)
    kappa = sigma * gamma - first
    group = lane // 32
    for source in range(64):
        number = numbers[source // 8][source % 8, 0]
        part = recv[source]
        mixed = part + kappa * pltpu.roll(part, 96, 1) - sigma * pltpu.roll(part, 64, 1)
        mixed = pltpu.roll(mixed, 32 * (number % 4), 1)
        pltpu.store(rows.at[number // 4], mixed, mask=group == number % 4)
    high, low = split(jnp.concatenate([rows[place] for place in range(16)], axis=1))
    both = jnp.concatenate([high, low], axis=0)
    base = 8 * lax.axis_index(XY)
    own = 16 * lax.axis_index("T") + 4 * lax.axis_index("Z")
    labels = [pick(recv[own + y], 101)[0:1] * 0.125 - base.astype(F32) for y in range(4)]
    turned = jnp.where(lane == row, sigma, jnp.where(lane == row + 8, kappa, 0.0))
    scalars = jnp.sum(turned, axis=0, keepdims=True)
    out = [[jnp.zeros((1, 128), F32) for _ in range(3)] for _ in range(4)]
    for half in range(2):
        begin = 128 * half
        held_high, held_low = split(inverse[begin : begin + 128])
        value = lax.dot_general(both, held_high, NT, preferred_element_type=F32)
        value = value[0:8] + value[8:16]
        value = value + lax.dot_general(high, held_low, NT, preferred_element_type=F32)
        rolled = turns(value)
        for place in range(4):
            packed = (*pack(rolled, place, row, lane), scalars)
            for y in range(4):
                for line in range(3):
                    out[y][line] = jnp.where(
                        labels[y] == float(4 * half + place), packed[line], out[y][line]
                    )
    for y in range(4):
        block = jnp.concatenate([*out[y], jnp.zeros((1, 128), F32)], axis=0)
        for side in range(4):
            for c in range(2):
                send[8 * side + 2 * y + c] = block


def last_kernel(recv, field, differ, image, image_two, vectors, solved, residual):
    lane = lax.broadcasted_iota(jnp.int32, (8, 128), 1)
    row = lax.broadcasted_iota(jnp.int32, (8, 128), 0)
    parts, sigmas, kappas = [], [], []
    for group in range(4):
        total = recv[8 * group]
        for other in range(1, 8):
            total = total + recv[8 * group + other]
        lines = jnp.where(row < 4, total[0:1], total[1:2])
        rolled = turns(lines)
        for right in range(1, 4):
            lines = jnp.where(row % 4 == right, rolled[right], lines)
        parts.append(lines)
        scalars = jnp.broadcast_to(total[2:3], (8, 128))
        sigmas.append(jnp.sum(jnp.where(lane == row, scalars, 0.0), axis=1, keepdims=True))
        kappas.append(jnp.sum(jnp.where(lane == row + 8, scalars, 0.0), axis=1, keepdims=True))
    correction = jnp.concatenate(parts, axis=0)[:, 0:32]
    sigma, kappa = jnp.concatenate(sigmas, axis=0), jnp.concatenate(kappas, axis=0)
    for site in range(2):
        b, u, w, q = field[site], differ[site], image[site], image_two[site]
        residual[site] = u + kappa * w - sigma * q
        solved[site] = (1.0 - kappa) * b + sigma * u + dot(correction, vectors[site], NN)


def call(kernel, scalars, arrays, outs, name, cost=None, scratch=()):
    return pl.pallas_call(
        kernel,
        out_shape=[jax.ShapeDtypeStruct(shape, kind) for shape, kind in outs],
        in_specs=[pl.BlockSpec(memory_space=pltpu.SMEM)] * len(scalars)
        + [pl.BlockSpec(memory_space=pltpu.VMEM)] * len(arrays),
        out_specs=[pl.BlockSpec(memory_space=pltpu.VMEM)] * len(outs),
        compiler_params=pltpu.CompilerParams(vmem_limit_bytes=16 * 1024 * 1024),
        cost_estimate=cost,
        scratch_shapes=scratch,
        name=name,
    )(*scalars, *arrays)


def halo(field):
    sides = []
    for axis, step in SIDES:
        sides.append(lax.ppermute(field, axis, [((i + step) % 8, i) for i in range(8)]))
    return sides


def body(right_side, stencil, restrict, aggregate, coarsest_inverse):
    field = right_side[0, 0, 0]
    vectors = restrict[0, 0, 0]
    local = (field.shape, F32)
    label = aggregate.reshape(2)
    (weights,) = call(
        prepare_kernel,
        (),
        (stencil[0, 0, 0],),
        (((2, 4, 256, 256), BF16),),
        "prepare",
        pl.CostEstimate(flops=1 << 20, bytes_accessed=1 << 23, transcendentals=0),
    )
    image, differ = call(
        first_kernel,
        (),
        (field, *halo(field), weights),
        (local, local),
        "first_image",
    )
    (early,) = call(
        early_kernel, (label,), (differ, image, vectors), (((32, 128), F32),), "early_part"
    )
    image_two, send = call(
        second_kernel,
        (),
        (differ, *halo(differ), weights, image, vectors, early),
        (local, ((8, 8, 128), F32)),
        "second_image",
    )
    recv = lax.all_to_all(send, BLOCK, 0, 0, tiled=True)
    (send,) = call(gather_kernel, (), (recv,), (((64, 8, 128), F32),), "block_sum")
    recv = lax.all_to_all(send, LATTICE, 0, 0, tiled=True)
    (send,) = call(
        coarse_kernel,
        (),
        (recv, coarsest_inverse),
        (((32, 4, 128), F32),),
        "coarse_solve",
        scratch=[pltpu.VMEM((16, 8, 128), F32)],
    )
    recv = lax.all_to_all(send, COLUMN, 0, 0, tiled=True)
    solved, residual = call(
        last_kernel,
        (),
        (recv, field, differ, image, image_two, vectors),
        (local, local),
        "last_update",
    )
    return solved[None, None, None], residual[None, None, None]


def solution(mesh):
    blocks = Mesh(mesh.devices.reshape(4, 2, 4, 2, 4, 2), ("T", "a", "Z", "b", "Y", "c"))
    spec = P(TA, GZ, XY)
    return jax.shard_map(
        body,
        mesh=blocks,
        in_specs=(spec, spec, spec, spec, P(XY)),
        out_specs=(spec, spec),
        check_vma=False,
    )
```
